32 devices in a mesh: fsdp: 4 (over z), ctx: 4 (over x, core), tp: 2 (over y).
Axes of the slice: x: 2, y: 2, z: 4, core: 2. Of those that a mesh axis runs over, the one named last changes fastest.
Arguments:
- tokens: bfloat16 [4, 1536, 2048], P('fsdp', 'ctx'), may hold values from -6 to 6
- seq_ids: int32 [4, 1536], P('fsdp'), may hold values from 0 to 2, never falling along the last dimension, each value on 1 to 768 neighbouring positions
- pic_starts: int32 [4, 3], P('fsdp'), may hold values from 0 to 1408, as said below
- pic_lengths: int32 [4, 3], P('fsdp'), may hold values from 128 to 256, as said below
- skip_mask: int32 [4, 1536], P('fsdp', 'ctx'), may hold values 0 or 1
- w_query: bfloat16 [2048, 2048], P('fsdp', 'tp'), may hold values from -0.125 to 0.125
- w_key: bfloat16 [2048, 512], P('fsdp', 'tp'), may hold values from -0.125 to 0.125
- w_value: bfloat16 [2048, 512], P('fsdp', 'tp'), may hold values from -0.125 to 0.125
- w_out: bfloat16 [2048, 2048], P('tp', 'fsdp'), may hold values from -1 to 1
- w_gate: bfloat16 [2048, 5632], P('fsdp', 'tp'), may hold values from -0.125 to 0.125
- w_up: bfloat16 [2048, 5632], P('fsdp', 'tp'), may hold values from -0.125 to 0.125
- w_down: bfloat16 [5632, 2048], P('tp', 'fsdp'), may hold values from -0.078125 to 0.078125
- gain_attn: bfloat16 [2048], P('fsdp'), may hold values from 0.25 to 1.75
- gain_ffn: bfloat16 [2048], P('fsdp'), may hold values from 0.25 to 1.75
- cotangent: bfloat16 [4, 1536, 2048], P('fsdp', 'ctx'), may hold values from -6 to 6
Outputs:
- output: bfloat16 [4, 1536, 2048], P('fsdp', 'ctx')
- input_grad: bfloat16 [4, 1536, 2048], P('fsdp', 'ctx')
- grad_query: float32 [2048, 2048], P('fsdp', 'tp')
- grad_key: float32 [2048, 512], P('fsdp', 'tp')
- grad_value: float32 [2048, 512], P('fsdp', 'tp')
- grad_out: float32 [2048, 2048], P('tp', 'fsdp')
- grad_gate: float32 [2048, 5632], P('fsdp', 'tp')
- grad_up: float32 [2048, 5632], P('fsdp', 'tp')
- grad_down: float32 [5632, 2048], P('tp', 'fsdp')
- grad_gain_attn: float32 [2048], P('fsdp')
- grad_gain_ffn: float32 [2048], P('fsdp')
The draws below stay inside these ranges and needn't reach their ends.
Inputs may be any that keep to these rules, and one draw needn't show every extreme that they name: `pic_starts`: picture p of a row (counting from 0) lies inside positions p * 2 * 256 to (p + 1) * 2 * 256 - 1, so pictures never intersect; it may start anywhere in that range where it fits. `pic_lengths`: every row has a picture of exactly 256 positions and another of exactly 128.
All inputs are finite; a program needn't handle non-finite values. No bound on the sum of `skip_mask` on one device may be relied on, other than what follows from the above.
Results may differ from the reference program's by a relative error of at most 0.022.
Values may be sent and summed in bfloat16 or wider, within the bound.
No kernel may reach another device: no remote copies, remote signals or barrier semaphores. Data moves between devices by JAX's collectives and lax.ppermute only.
A program may use at most 256 MiB of HBM per device.

```python
import math
import jax
import jax.numpy as jnp
import numpy as np
from jax import lax

D = 2048
HEADS = 16
KV_HEADS = 4
HEAD = 128
FF = 5632
PIC_LEN = 256
DOCS = 3
SEQ = 1536
ROWS = 4
PICS = 3


def picture_layout(key):
    base_key = jax.random.fold_in(key, 7)
    keys_list = jax.random.split(base_key, 6)
    slot_index = jnp.arange(PICS, dtype=jnp.int32)[None, :]
    row_index = jnp.arange(ROWS, dtype=jnp.int32)[:, None]
    low_row = jax.random.randint(keys_list[4], (), 0, ROWS)
    high_row = jax.random.randint(keys_list[5], (), 0, ROWS)
    is_high = row_index == high_row
    full_any = jax.random.randint(keys_list[1], (ROWS, 1), 0, PICS)
    half_any = (full_any + 1 + jax.random.randint(keys_list[2], (ROWS, 1), 0, PICS - 1)) % PICS
    full_slot = jnp.where(is_high, full_any % (PICS - 1), full_any)
    half_slot = jnp.where(is_high, PICS - 1, half_any)
    lengths = jax.random.randint(keys_list[0], (ROWS, PICS), PIC_LEN // 2, PIC_LEN + 1)
    lengths = jnp.where(slot_index == full_slot, PIC_LEN, lengths)
    lengths = jnp.where(slot_index == half_slot, PIC_LEN // 2, lengths)
    slot_width = SEQ // PICS
    free_room = slot_width - lengths + 1
    offsets = jax.random.randint(keys_list[3], (ROWS, PICS), 0, free_room)
    offsets = jnp.where((row_index == low_row) & (slot_index == 0), 0, offsets)
    offsets = jnp.where(is_high & (slot_index == PICS - 1), free_room - 1, offsets)
    starts = slot_index * slot_width + offsets
    return (starts.astype(jnp.int32), lengths.astype(jnp.int32))


def draw_pic_starts(key, part):
    return picture_layout(key)[0]


def draw_pic_lengths(key, part):
    return picture_layout(key)[1]


def plant(result, own_key, low, high):
    extent = result.shape
    spot = [jax.random.randint(jax.random.fold_in(own_key, axis), (), 0, extent[axis]) for axis in range(len(extent))]
    result = result.at[tuple(spot)].set(low)
    longest = extent.index(max(extent))
    spot[longest] = (spot[longest] + 1) % extent[longest]
    return result.at[tuple(spot)].set(high)


def steps_of(stream_key, shape, shards, least, high):
    def one(dim, shards_of):
        heights = jax.random.uniform(jax.random.fold_in(jax.random.fold_in(stream_key, 6), dim), (shards_of,), jnp.float32, least / len(shards), high / len(shards))
        return jnp.repeat(jnp.exp(heights), shape[dim] // shards_of).reshape((-1,) + (1,) * (len(shape) - dim - 1))

    level = one(*shards[0])
    for cut in shards[1:]:
        level = level * one(*cut)
    return level


def length_profile(amount, total, most, lean):
    weights = [(1 << 20) // math.isqrt(grade ** lean) + 1 for grade in range(2, amount + 1)]
    surplus, holding = total - most - (amount - 1), [1] * (amount - 1)
    while surplus > 0:
        movable = [i for i in range(amount - 1) if holding[i] < most]
        whole, left = sum([weights[i] for i in movable]), surplus
        for i in movable:
            more = min(most - holding[i], max(1, left * weights[i] // whole), surplus)
            holding[i] = holding[i] + more
            surplus = surplus - more
    return np.array([most] + holding)


def uneven(stream_key, number_of, total, most, skew):
    if number_of == 2:
        one = jax.random.randint(stream_key, (), max(1, total - most), min(most, total - 1) + 1)
        return jnp.stack([one, total - one])
    sizes = jnp.asarray(length_profile(number_of, total, most, skew), jnp.int32)
    twos = (number_of - 1) // 2
    donor, sink = sizes[1:1 + 2 * twos:2], sizes[2:2 + 2 * twos:2]
    slack = jnp.minimum(donor - 1, most - sink)
    moved = jax.random.randint(jax.random.fold_in(stream_key, 1), (twos,), 0, 1 << 20) % (slack + 1)
    sizes = sizes.at[1:1 + 2 * twos:2].set(donor - moved).at[2:2 + 2 * twos:2].set(sink + moved)
    return sizes[jax.random.permutation(jax.random.fold_in(stream_key, 2), number_of)]


def normal_values(key, extent, scale, bound, cuts=(), held_as=jnp.bfloat16):
    entries = jax.random.normal(key, extent, jnp.float32) * scale
    if len(cuts) > 0:
        entries = steps_of(key, extent, cuts, -0.22, 0.18) * entries
    return jnp.clip(entries, min=-bound, max=bound).astype(held_as)


def setup_inputs(seed: int = 0) -> dict:
    seeds = jax.random.split(jax.random.key(seed), 16)
    return {
        "tokens": normal_values(seeds[0], (ROWS, SEQ, D), 1.0, 6.0, ((0, 4), (1, 4))),
        "seq_ids": jax.vmap(lambda own: jnp.searchsorted(jnp.cumsum(uneven(own, DOCS, SEQ, SEQ // 2, 0)), jnp.arange(SEQ), side="right"))(jax.random.split(seeds[1], ROWS)).reshape((ROWS, SEQ)).astype(jnp.int32),
        "pic_starts": draw_pic_starts(jax.random.fold_in(seeds[15], 71), 0),
        "pic_lengths": draw_pic_lengths(jax.random.fold_in(seeds[15], 71), 0),
        "skip_mask": plant((jax.random.randint(seeds[4], (ROWS, SEQ), 0, 4) < 3).astype(jnp.int32), jax.random.fold_in(seeds[4], 1), 0, 1),
        "w_query": normal_values(seeds[5], (D, HEADS * HEAD), D ** -0.5, 0.125, ((0, 4), (1, 2))),
        "w_key": normal_values(seeds[6], (D, KV_HEADS * HEAD), D ** -0.5, 0.125, ((0, 4), (1, 2))),
        "w_value": normal_values(seeds[7], (D, KV_HEADS * HEAD), D ** -0.5, 0.125, ((0, 4), (1, 2))),
        "w_out": normal_values(seeds[8], (HEADS * HEAD, D), (HEADS * HEAD // 64) ** -0.5, 1.0, ((0, 2), (1, 4))),
        "w_gate": normal_values(seeds[9], (D, FF), D ** -0.5, 0.125, ((0, 4), (1, 2))),
        "w_up": normal_values(seeds[10], (D, FF), D ** -0.5, 0.125, ((0, 4), (1, 2))),
        "w_down": normal_values(seeds[11], (FF, D), FF ** -0.5, 0.078125, ((0, 2), (1, 4))),
        "gain_attn": jnp.clip(1.0 + 0.15 * jax.random.normal(seeds[12], (D,), jnp.float32), 0.25, 1.75).astype(jnp.bfloat16),
        "gain_ffn": jnp.clip(1.0 + 0.15 * jax.random.normal(seeds[13], (D,), jnp.float32), 0.25, 1.75).astype(jnp.bfloat16),
        "cotangent": normal_values(seeds[14], (ROWS, SEQ, D), 1.0, 6.0, ((0, 4), (1, 4))),
    }


norm_eps = 1e-05
rope_base = 10000.0

@jax.custom_vjp
def low(v):
    return lax.optimization_barrier(v.astype(jnp.bfloat16)).astype(jnp.float32)

@jax.custom_vjp
def low_back(v):
    return v

def low_keep(v):
    return (low(v), None)

def low_pass(kept, grad):
    return (grad,)

def back_keep(v):
    return (v, None)

def back_low(kept, grad):
    return (low(grad),)
low.defvjp(low_keep, low_pass)
low_back.defvjp(back_keep, back_low)

def rms_norm(values_in, gain):
    return values_in * lax.rsqrt(lax.optimization_barrier(jnp.mean(values_in * values_in, axis=-1, keepdims=True)) + norm_eps) * gain

def rotate(values_in, positions, sign):
    half_width = values_in.shape[-1] // 2
    frequency = jnp.power(rope_base, -jnp.arange(half_width, dtype=jnp.float32) * 2.0 / values_in.shape[-1])
    angles = positions.astype(jnp.float32)[:, None] * frequency[None, :]
    cosine = jnp.cos(angles)[:, None, :]
    sine_val = sign * jnp.sin(angles)[:, None, :]
    first_half = values_in[..., :half_width]
    second = values_in[..., half_width:]
    return jnp.concatenate([first_half * cosine - second * sine_val, second * cosine + first_half * sine_val], axis=-1)

def picture_ids(starts, lengths, positions):
    inside = (positions[:, None] >= starts[None, :]) & (positions[:, None] < starts[None, :] + lengths[None, :])
    numbers = jnp.arange(1, starts.shape[0] + 1, dtype=jnp.int32)
    return lax.optimization_barrier(jnp.sum(jnp.where(inside, numbers[None, :], 0), axis=1)).astype(jnp.int32)

def allowed_mask(query_pos, key_pos, query_doc, key_doc, query_pic, key_pic):
    same_doc = query_doc[:, None] == key_doc[None, :]
    causal = key_pos[None, :] <= query_pos[:, None]
    picture = (query_pic[:, None] == key_pic[None, :]) & (query_pic[:, None] > 0)
    return same_doc & (causal | picture)

def row_forward(inputs_f, w_query, w_key, w_value, w_out, w_gate, w_up, w_down, gain_attn, gain_ffn, doc_ids, starts, lengths, keep_rows):
    highest = lax.Precision.HIGHEST
    positions = jnp.arange(SEQ, dtype=jnp.int32)
    pic_ids = picture_ids(starts, lengths, positions)
    normed_one = low(rms_norm(inputs_f, gain_attn))
    query_pre = low_back(jnp.dot(normed_one, w_query, precision=highest))
    key_pre = low_back(jnp.dot(normed_one, w_key, precision=highest))
    value_pre = low_back(jnp.dot(normed_one, w_value, precision=highest))
    queries = low(rotate(query_pre.reshape(SEQ, HEADS, HEAD), positions, 1.0) * (1.0 / math.sqrt(HEAD)))
    keys = low(rotate(key_pre.reshape(SEQ, KV_HEADS, HEAD), positions, 1.0))
    values = low(value_pre.reshape(SEQ, KV_HEADS, HEAD))
    group_size = HEADS // KV_HEADS
    block_rows = min(512, SEQ)
    blocks = SEQ // block_rows

    def one_block(pieces):
        query_block, pos_block, doc_block, pic_block = pieces
        grouped = query_block.reshape(block_rows, KV_HEADS, group_size, HEAD)
        scores = low_back(jnp.einsum('qhgd,khd->hgqk', grouped, keys, precision=highest))
        allowed = allowed_mask(pos_block, positions, doc_block, doc_ids, pic_block, pic_ids)
        masked = jnp.where(allowed[None, None], scores, -1e+30)
        soft_b = low(jax.nn.softmax(masked, axis=-1))
        head_block = jnp.einsum('hgqk,khd->qhgd', soft_b, values, precision=highest)
        return head_block.reshape(block_rows, HEADS * HEAD)
    head_outs = lax.map(jax.checkpoint(one_block), (queries.reshape(blocks, block_rows, HEADS, HEAD), positions.reshape(blocks, block_rows), doc_ids.reshape(blocks, block_rows), pic_ids.reshape(blocks, block_rows)))
    head_out = low(low_back(head_outs.reshape(SEQ, HEADS * HEAD)))
    attn = low_back(jnp.dot(head_out, w_out, precision=highest))
    keep_f = keep_rows.astype(jnp.float32)[:, None]
    mid = inputs_f + keep_f * attn
    normed_two = low(rms_norm(mid, gain_ffn))
    gate_act = low_back(jnp.dot(normed_two, w_gate, precision=highest))
    up_act = low_back(jnp.dot(normed_two, w_up, precision=highest))
    hidden = low(jax.nn.silu(gate_act) * up_act)
    ffn = low_back(jnp.dot(hidden, w_down, precision=highest))
    return mid + keep_f * ffn

def reference(tokens, seq_ids, pic_starts, pic_lengths, skip_mask, w_query, w_key, w_value, w_out, w_gate, w_up, w_down, gain_attn, gain_ffn, cotangent):
    params = tuple((w.astype(jnp.float32) for w in (w_query, w_key, w_value, w_out, w_gate, w_up, w_down, gain_attn, gain_ffn)))

    def scan_step(running, row_data):
        row_tokens, row_docs, row_starts, row_lengths, row_keep, row_cot = row_data

        def forward(inputs_f, p_query, p_key, p_value, p_out, p_gate, p_up, p_down, p_gain_one, p_gain_two):
            return row_forward(inputs_f, p_query, p_key, p_value, p_out, p_gate, p_up, p_down, p_gain_one, p_gain_two, row_docs, row_starts, row_lengths, row_keep)
        row_out, pullback = jax.vjp(forward, row_tokens.astype(jnp.float32), params[0], params[1], params[2], params[3], params[4], params[5], params[6], params[7], params[8])
        grad_list = pullback(row_cot.astype(jnp.float32))
        updated = tuple((acc + grad for acc, grad in zip(running, grad_list[1:])))
        return (updated, (row_out.astype(jnp.bfloat16), grad_list[0].astype(jnp.bfloat16)))
    start_sums = tuple((jnp.zeros(w.shape, jnp.float32) for w in params))
    totals_all, (outputs, input_grads) = lax.scan(scan_step, start_sums, (tokens, seq_ids, pic_starts, pic_lengths, skip_mask, cotangent))
    return (outputs, input_grads, totals_all[0], totals_all[1], totals_all[2], totals_all[3], totals_all[4], totals_all[5], totals_all[6], totals_all[7], totals_all[8])
```

```python
import math

import jax
import jax.numpy as jnp
from jax import lax
from jax.sharding import PartitionSpec as P

HEAD = 128
norm_eps = 1e-05
rope_base = 10000.0
F32 = jnp.float32
BF16 = jnp.bfloat16


def dot(a, b, ca, cb):
    return lax.dot_general(a, b, (((ca,), (cb,)), ((), ())), preferred_element_type=F32)


def rope_tables(positions):
    half_width = HEAD // 2
    frequency = jnp.power(rope_base, -jnp.arange(half_width, dtype=F32) * 2.0 / HEAD)
    angles = positions.astype(F32)[:, None] * frequency[None, :]
    return jnp.cos(angles), jnp.sin(angles)


def rotate(u, cosine, sine):
    half_width = HEAD // 2
    parts = []
    for head in range(u.shape[1] // HEAD):
        first = u[:, head * HEAD : head * HEAD + half_width]
        second = u[:, head * HEAD + half_width : (head + 1) * HEAD]
        parts += [first * cosine - second * sine, second * cosine + first * sine]
    return jnp.concatenate(parts, axis=1)


def picture_ids(starts, lengths, positions):
    inside = (positions[:, None] >= starts[None, :]) & (
        positions[:, None] < starts[None, :] + lengths[None, :]
    )
    numbers = jnp.arange(1, starts.shape[0] + 1, dtype=jnp.int32)
    return jnp.sum(jnp.where(inside, numbers[None, :], 0), axis=1)


def allowed_mask(query_pos, key_pos, query_doc, key_doc, query_pic, key_pic):
    same_doc = query_doc[:, None] == key_doc[None, :]
    causal = key_pos[None, :] <= query_pos[:, None]
    picture = (query_pic[:, None] == key_pic[None, :]) & (query_pic[:, None] > 0)
    return same_doc & (causal | picture)


def norm_back(d_normed, hat, inv_rms, gain):
    scaled = d_normed * gain
    return inv_rms * (scaled - hat * jnp.mean(scaled * hat, axis=-1, keepdims=True))


def far(v):
    return lax.ppermute(v, "ctx", [(i, i ^ 2) for i in range(4)])


def near(v):
    return lax.ppermute(v, "ctx", [(i, i ^ 1) for i in range(4)])


def side(v):
    return lax.ppermute(v, "tp", [(0, 1), (1, 0)])


def spread(v):
    n, w = v.shape
    left, right = v[:, : w // 2], v[:, w // 2 :]
    left_far = far(left)
    right_side = side(right)
    left_two = side(jnp.concatenate([left, left_far], axis=0))
    right_two = far(jnp.concatenate([right, right_side], axis=0))
    left_all = jnp.concatenate([left, left_two[:n], left_far, left_two[n:]], axis=0)
    right_all = jnp.concatenate([right, right_side, right_two], axis=0)
    mine = jnp.concatenate([left_all, right_all], axis=1)
    return jnp.concatenate([mine, near(mine)], axis=0)


def collect(p):
    n, w = p.shape[0] // 8, p.shape[1]
    both = p[: 4 * n].astype(F32) + near(p[4 * n :]).astype(F32)
    both = both.astype(BF16)
    left, right = both[:, : w // 2], both[:, w // 2 :].reshape(2, 2, n, w // 2)
    left_far = far(left[2 * n :])
    right_side = side(right[:, 1].reshape(2 * n, w // 2))
    left = (left[: 2 * n].astype(F32) + left_far.astype(F32)).astype(BF16)
    right = (right[:, 0].reshape(2 * n, w // 2).astype(F32) + right_side.astype(F32)).astype(BF16)
    left_side = side(left[n:])
    right_far = far(right[n:])
    return jnp.concatenate(
        [
            left[:n].astype(F32) + left_side.astype(F32),
            right[:n].astype(F32) + right_far.astype(F32),
        ],
        axis=1,
    )


def both_sides(v, t):
    other = side(v)
    return jnp.where(
        t == 0, jnp.concatenate([v, other], axis=0), jnp.concatenate([other, v], axis=0)
    )


def ctx_rows(v, c):
    n = v.shape[0]
    two = jnp.stack([v, far(v)])
    other = near(two)
    out = jnp.zeros((4, n, v.shape[1]), v.dtype)
    for bits, piece in ((0, two[0]), (2, two[1]), (1, other[0]), (3, other[1])):
        out = lax.dynamic_update_slice(out, piece[None], (c ^ bits, 0, 0))
    return out


def swap_halves(v):
    n = v.shape[0] // 2
    return jnp.concatenate([v[n:], v[:n]], axis=0)


def body(
    tokens,
    seq_ids,
    pic_starts,
    pic_lengths,
    skip_mask,
    w_query,
    w_key,
    w_value,
    w_out,
    w_gate,
    w_up,
    w_down,
    gain_attn,
    gain_ffn,
    cotangent,
):
    tok_rows = tokens.shape[1]
    width = tokens.shape[2]
    own = tok_rows // 2
    seq_len = seq_ids.shape[1]
    c = lax.axis_index("ctx")
    t = lax.axis_index("tp")
    core = c & 1
    q_cols = w_query.shape[1] // 4
    heads = q_cols // HEAD
    ff = w_gate.shape[1] // 4
    query_scale = 1.0 / math.sqrt(HEAD)

    wq_t = lax.dynamic_slice_in_dim(w_query, c * q_cols, q_cols, 1).T
    w_kv = jnp.where(core == 0, w_key, w_value)
    wkv_t = lax.dynamic_slice_in_dim(w_kv, (c >> 1) * HEAD, HEAD, 1).T
    gains = jnp.concatenate(
        [gain_attn[None], gain_ffn[None], jnp.zeros((14, gain_attn.shape[0]), BF16)], axis=0
    )
    first = lax.all_gather(
        jnp.concatenate([wq_t, wkv_t, gains], axis=0), "fsdp", axis=1, tiled=True
    )
    qkv_cols = q_cols + HEAD
    wqkv = first[:qkv_cols]
    gain_one = first[qkv_cols].astype(F32)
    gain_two = first[qkv_cols + 1].astype(F32)
    wo = lax.all_gather(
        lax.dynamic_slice_in_dim(w_out, c * q_cols, q_cols, 0), "fsdp", axis=1, tiled=True
    )
    wg_t = lax.dynamic_slice_in_dim(w_gate, c * ff, ff, 1).T
    wu_t = lax.dynamic_slice_in_dim(w_up, c * ff, ff, 1).T
    wgu = lax.all_gather(jnp.concatenate([wg_t, wu_t], axis=0), "fsdp", axis=1, tiled=True)
    wd = lax.all_gather(
        lax.dynamic_slice_in_dim(w_down, c * ff, ff, 0), "fsdp", axis=1, tiled=True
    )

    x_own_b = lax.dynamic_slice_in_dim(tokens[0], t * own, own, 0)
    x_own = x_own_b.astype(F32)
    keep_own = lax.dynamic_slice_in_dim(skip_mask[0], t * own, own, 0).astype(F32)[:, None]
    dy_own = lax.dynamic_slice_in_dim(cotangent[0], t * own, own, 0).astype(F32)
    d_ffn_own = (keep_own * dy_own).astype(BF16)

    pos_list = []
    for block in range(8):
        near_bit, far_bit, side_bit = block >> 2, (block >> 1) & 1, block & 1
        start = (c ^ (near_bit + 2 * far_bit)) * tok_rows + (t ^ side_bit) * own
        pos_list.append(start)
    positions = jnp.concatenate([s + jnp.arange(own, dtype=jnp.int32) for s in pos_list])
    docs = jnp.concatenate([lax.dynamic_slice_in_dim(seq_ids[0], s, own, 0) for s in pos_list])
    pics = picture_ids(pic_starts[0], pic_lengths[0], positions)
    allowed = allowed_mask(positions, positions, docs, docs, pics, pics)
    cosine, sine = rope_tables(positions)

    x_all = spread(x_own_b).astype(F32)
    inv_all = lax.rsqrt(jnp.mean(x_all * x_all, axis=-1, keepdims=True) + norm_eps)
    n1 = (x_all * inv_all * gain_one).astype(BF16)
    qkv_pre = dot(n1, wqkv, 1, 1)
    queries = (rotate(qkv_pre[:, :q_cols], cosine, sine) * query_scale).astype(BF16)
    kv_pre = qkv_pre[:, q_cols:]
    kv_own = jnp.where(core == 0, rotate(kv_pre, cosine, sine), kv_pre).astype(BF16)
    kv_other = swap_halves(near(kv_own))
    keys = jnp.where(core == 0, kv_own, kv_other)
    values = jnp.where(core == 0, kv_other, kv_own)
    q_heads = queries.reshape(seq_len, heads, HEAD)
    scores = jnp.einsum("qhd,kd->hqk", q_heads, keys, preferred_element_type=F32)
    masked = jnp.where(allowed[None], scores, -1e30)
    row_max = jnp.max(masked, axis=-1, keepdims=True)
    exp_scores = jnp.exp(masked - row_max)
    row_total = jnp.sum(exp_scores, axis=-1, keepdims=True)
    soft_b = (exp_scores / row_total).astype(BF16)
    log_total = row_max + jnp.log(row_total)
    head_out = (
        jnp.einsum("hqk,kd->qhd", soft_b, values, preferred_element_type=F32)
        .reshape(seq_len, q_cols)
        .astype(BF16)
    )
    attn = collect(dot(head_out, wo, 1, 0).astype(BF16))
    mid = x_own + keep_own * attn
    inv_two = lax.rsqrt(jnp.mean(mid * mid, axis=-1, keepdims=True) + norm_eps)
    hat_two = mid * inv_two
    n2 = spread((hat_two * gain_two).astype(BF16))

    d_ffn = spread(d_ffn_own)
    gu = dot(wgu, n2, 1, 1)
    gate, up = gu[:ff], gu[ff:]
    sig = jax.nn.sigmoid(gate)
    hidden = (gate * sig * up).astype(BF16)
    d_hidden = dot(wd, d_ffn, 1, 1)
    d_gate = (d_hidden * up * sig * (1.0 + gate * (1.0 - sig))).astype(BF16)
    d_up = (d_hidden * (gate * sig)).astype(BF16)
    d_gu = jnp.concatenate([d_gate, d_up], axis=0)
    d_n2 = collect(dot(d_gu, wgu, 0, 0).astype(BF16))
    grad_gu = dot(d_gu, n2, 1, 0).astype(BF16)
    grad_down = dot(hidden, d_ffn, 1, 0).astype(BF16)
    shard_gu = lax.psum_scatter(grad_gu, "fsdp", scatter_dimension=1, tiled=True)
    shard_down = lax.psum_scatter(grad_down, "fsdp", scatter_dimension=1, tiled=True)
    ffn = collect(dot(hidden, wd, 0, 0).astype(BF16))
    output = both_sides((mid + keep_own * ffn).astype(BF16), t)

    d_mid = dy_own + norm_back(d_n2, hat_two, inv_two, gain_two)
    d_attn = spread((keep_own * d_mid).astype(BF16))
    grad_out = dot(head_out, d_attn, 0, 0).astype(BF16)
    shard_out = lax.psum_scatter(grad_out, "fsdp", scatter_dimension=1, tiled=True)
    d_head = dot(d_attn, wo, 1, 1).astype(BF16).reshape(seq_len, heads, HEAD)
    scores = jnp.einsum("qhd,kd->hqk", q_heads, keys, preferred_element_type=F32)
    soft = jnp.where(allowed[None], jnp.exp(scores - log_total), 0.0)
    d_soft = jnp.einsum("qhd,kd->hqk", d_head, values, preferred_element_type=F32)
    delta = jnp.sum(soft * d_soft, axis=-1, keepdims=True)
    d_scores = (soft * (d_soft - delta)).astype(BF16)
    d_queries = jnp.einsum("hqk,kd->qhd", d_scores, keys, preferred_element_type=F32)
    d_keys = jnp.einsum("hqk,qhd->kd", d_scores, q_heads, preferred_element_type=F32)
    d_values = jnp.einsum("hqk,qhd->kd", soft.astype(BF16), d_head, preferred_element_type=F32)
    sent = swap_halves(near(jnp.where(core == 0, d_values, d_keys).astype(BF16)))
    d_kv = jnp.where(core == 0, d_keys, d_values) + sent.astype(F32)
    d_kv_pre = jnp.where(core == 0, rotate(d_kv, cosine, -sine), d_kv)
    d_query_pre = rotate(d_queries.reshape(seq_len, q_cols), cosine, -sine) * query_scale
    d_qkv = jnp.concatenate([d_query_pre.astype(BF16), d_kv_pre.astype(BF16)], axis=1)
    grad_qkv = dot(d_qkv, n1, 0, 0).astype(BF16)
    shard_qkv = lax.psum_scatter(grad_qkv, "fsdp", scatter_dimension=1, tiled=True)
    d_n1 = collect(dot(d_qkv, wqkv, 1, 0).astype(BF16))
    inv_one = lax.rsqrt(jnp.mean(x_own * x_own, axis=-1, keepdims=True) + norm_eps)
    hat_one = x_own * inv_one
    input_grad = both_sides(
        (d_mid + norm_back(d_n1, hat_one, inv_one, gain_one)).astype(BF16), t
    )

    gain_grads = lax.psum(
        jnp.stack([jnp.sum(d_n1 * hat_one, axis=0), jnp.sum(d_n2 * hat_two, axis=0)]),
        ("fsdp", "ctx", "tp"),
    )
    shard_width = gain_attn.shape[0]
    gain_grads = lax.dynamic_slice_in_dim(
        gain_grads, lax.axis_index("fsdp") * shard_width, shard_width, 1
    )

    all_gu = ctx_rows(shard_gu, c)
    all_down = ctx_rows(shard_down, c).reshape(4 * ff, -1)
    all_out = ctx_rows(shard_out, c).reshape(4 * q_cols, -1)
    all_qkv = ctx_rows(shard_qkv, c)
    grad_kv = all_qkv[:, q_cols:].reshape(2, 2, HEAD, -1)
    return (
        output[None],
        input_grad[None],
        all_qkv[:, :q_cols].reshape(4 * q_cols, -1).T.astype(F32),
        grad_kv[:, 0].reshape(2 * HEAD, -1).T.astype(F32),
        grad_kv[:, 1].reshape(2 * HEAD, -1).T.astype(F32),
        all_out.astype(F32),
        all_gu[:, :ff].reshape(4 * ff, -1).T.astype(F32),
        all_gu[:, ff:].reshape(4 * ff, -1).T.astype(F32),
        all_down.astype(F32),
        gain_grads[0],
        gain_grads[1],
    )


def solution(mesh):
    placed = (
        P("fsdp", "ctx", None),
        P("fsdp", None),
        P("fsdp", None),
        P("fsdp", None),
        P("fsdp", "ctx"),
        P("fsdp", "tp"),
        P("fsdp", "tp"),
        P("fsdp", "tp"),
        P("tp", "fsdp"),
        P("fsdp", "tp"),
        P("fsdp", "tp"),
        P("tp", "fsdp"),
        P("fsdp"),
        P("fsdp"),
        P("fsdp", "ctx", None),
    )
    return jax.shard_map(
        body,
        mesh=mesh,
        in_specs=placed,
        out_specs=(
            P("fsdp", "ctx", None),
            P("fsdp", "ctx", None),
            P("fsdp", "tp"),
            P("fsdp", "tp"),
            P("fsdp", "tp"),
            P("tp", "fsdp"),
            P("fsdp", "tp"),
            P("fsdp", "tp"),
            P("tp", "fsdp"),
            P("fsdp"),
            P("fsdp"),
        ),
        check_vma=False,
    )
```

```python
import functools
import math

import jax
import jax.numpy as jnp
from jax import lax
from jax.experimental import pallas as pl
from jax.experimental.pallas import tpu as pltpu
from jax.sharding import PartitionSpec as P

HEAD = 128
norm_eps = 1e-05
rope_base = 10000.0
F32 = jnp.float32
BF16 = jnp.bfloat16
ANY_VMEM = pl.BlockSpec(memory_space=pltpu.VMEM)
ANY_SMEM = pl.BlockSpec(memory_space=pltpu.SMEM)


def dot(a, b, ca, cb):
    return lax.dot_general(a, b, (((ca,), (cb,)), ((), ())), preferred_element_type=F32)


def after(v, *others):
    return lax.optimization_barrier((v,) + others)[0] if others else v


def fenced(flag, stage, *values):
    shapes = jax.eval_shape(stage, *values)

    def empty(*_):
        return jax.tree.map(lambda a: jnp.zeros(a.shape, a.dtype), shapes)

    return lax.cond(flag, stage, empty, *values)


def norm_back(d_normed, hat, inv_rms, gain):
    scaled = d_normed * gain
    return inv_rms * (scaled - hat * jnp.mean(scaled * hat, axis=-1, keepdims=True))


def far(v):
    return lax.ppermute(v, "ctx", [(i, i ^ 2) for i in range(4)])


def near(v):
    return lax.ppermute(v, "ctx", [(i, i ^ 1) for i in range(4)])


def side(v):
    return lax.ppermute(v, "tp", [(0, 1), (1, 0)])


def join_kernel(count, *refs):
    pieces, out_ref, sem = refs[:count], refs[-2], refs[-1]
    copies, row = [], 0
    for k, piece in enumerate(pieces):
        n = piece.shape[0]
        copies.append(pltpu.make_async_copy(piece, out_ref.at[pl.ds(row, n), :], sem.at[k]))
        copies[-1].start()
        row += n
    for copy in copies:
        copy.wait()


def join(*pieces, others=()):
    rows = sum(p.shape[0] for p in pieces)
    return pl.pallas_call(
        functools.partial(join_kernel, len(pieces)),
        out_shape=jax.ShapeDtypeStruct((rows, pieces[0].shape[1]), pieces[0].dtype),
        in_specs=[pl.BlockSpec(memory_space=pl.ANY)] * (len(pieces) + len(others)),
        out_specs=ANY_VMEM,
        scratch_shapes=[pltpu.SemaphoreType.DMA((len(pieces),))],
        name="join",
    )(*pieces, *others)


def spread_start(v):
    h = v.shape[0] // 2
    one, two = v[:h], v[h:]
    return one, two, far(one), side(two), side(one), far(two)


def spread_more(parts):
    one, two, one_far, two_side, one_side, two_far = parts
    return one_far, two_side, one_side, two_far, side(one_far), far(two_side)


def spread_join(ready, others=()):
    one, two, one_far, two_side, one_side, two_far, one_both, two_both = ready
    return join(one, one_far, one_side, one_both, two, two_side, two_far, two_both, others=others)


def spread(v, others=()):
    parts = spread_start(v)
    mine = spread_join(parts[:2] + spread_more(parts), others)
    return mine, near(mine)


def arrival_starts(c, t, tok_rows):
    own = tok_rows // 2
    starts = []
    for near_bit in range(2):
        for second in range(2):
            order = ((0, 0), (1, 0), (0, 1), (1, 1)) if second == 0 else ((0, 0), (0, 1), (1, 0), (1, 1))
            for far_bit, side_bit in order:
                ctx = c ^ (near_bit + 2 * far_bit)
                starts.append(ctx * tok_rows + (t ^ side_bit) * own + second * (own // 2))
    return starts


def collect_split(both):
    h = both.shape[0] // 8
    one = both[: 4 * h].reshape(2, 2, h, -1)
    two = both[4 * h :].reshape(2, 2, h, -1)
    return [v[:, k].reshape(2 * h, -1) for k in range(2) for v in (one, two)]


def collect_send(split):
    one, two, one_sent, two_sent = split
    return one, two, far(one_sent), side(two_sent)


def collect_first(both):
    return collect_send(collect_split(both))


def collect_second(state):
    one, two, one_far, two_side = state
    return add(one, one_far), add(two, two_side)


def collect_start(p_mine, p_other):
    return collect_second(collect_first(join_cores(p_mine, p_other)))


def join_cores(p_mine, p_other):
    return add(lax.optimization_barrier(p_mine), near(p_other))


def collect_end(state):
    one, two = state
    h = one.shape[0] // 2
    one_side = side(one[h:])
    two_far = far(two[h:])
    return jnp.concatenate(
        [
            one[:h].astype(F32) + one_side.astype(F32),
            two[:h].astype(F32) + two_far.astype(F32),
        ],
        axis=0,
    )


def collect(p_mine, p_other):
    return collect_end(collect_start(p_mine, p_other))


def in_order(v, other, t):
    return jnp.where(
        t == 0, jnp.concatenate([v, other], axis=0), jnp.concatenate([other, v], axis=0)
    )


def gather_whole(v):
    return lax.all_gather(v, "fsdp", axis=1, tiled=True)


def scatter_whole(g):
    return lax.psum_scatter(g, "fsdp", scatter_dimension=1, tiled=True)


def add(a, b):
    return (a.astype(F32) + b.astype(F32)).astype(BF16)


def pack_first_kernel(at_ref, wq_ref, wk_ref, wv_ref, wo_ref, one_ref, two_ref, out_ref):
    q_cols = wq_ref.shape[1]
    qkv = q_cols + HEAD
    out_ref[:q_cols, :] = wq_ref[...].astype(F32).T.astype(BF16)
    w_kv = jnp.where(at_ref[1] == 0, wk_ref[...].astype(F32), wv_ref[...].astype(F32))
    out_ref[q_cols:qkv, :] = w_kv.T.astype(BF16)
    row = lax.broadcasted_iota(jnp.int32, (16, out_ref.shape[1]), 0)
    one, two = one_ref[...].astype(F32)[None, :], two_ref[...].astype(F32)[None, :]
    out_ref[qkv : qkv + 16, :] = jnp.where(row == 0, one, jnp.where(row == 1, two, 0.0)).astype(BF16)
    out_ref[qkv + 16 :, :] = wo_ref[...]


def pack_first(at, w_query, w_key, w_value, w_out, gain_one, gain_two):
    depth = w_query.shape[0]
    q_cols = w_query.shape[1] // 4
    rows = 2 * q_cols + HEAD + 16
    gain = pl.BlockSpec((depth,), lambda i, at: (0,))
    return pl.pallas_call(
        pack_first_kernel,
        out_shape=jax.ShapeDtypeStruct((rows, depth), BF16),
        grid_spec=pltpu.PrefetchScalarGridSpec(
            num_scalar_prefetch=1,
            grid=(1,),
            in_specs=[
                pl.BlockSpec((depth, q_cols), lambda i, at: (0, at[0])),
                pl.BlockSpec((depth, HEAD), lambda i, at: (0, at[2])),
                pl.BlockSpec((depth, HEAD), lambda i, at: (0, at[2])),
                pl.BlockSpec((q_cols, depth), lambda i, at: (at[0], 0)),
                gain,
                gain,
            ],
            out_specs=pl.BlockSpec((rows, depth), lambda i, at: (0, 0)),
        ),
        name="pack_first",
    )(at, w_query, w_key, w_value, w_out, gain_one, gain_two)


def turn(u, cosine, sine):
    return u * cosine + pltpu.roll(u, HEAD // 2, 1) * sine


def qkv_kernel(heads, core_ref, x_ref, w_ref, gain_ref, cos_ref, sin_ref, n1_ref, q_ref, kv_ref):
    x = x_ref[...].astype(F32)
    inv = lax.rsqrt(jnp.mean(x * x, axis=-1, keepdims=True) + norm_eps)
    n1 = (x * inv * gain_ref[0:1, :].astype(F32)).astype(BF16)
    n1_ref[...] = n1
    pre = dot(n1, w_ref[...], 1, 1)
    cosine, sine = cos_ref[...], sin_ref[...]
    scale = 1.0 / math.sqrt(HEAD)
    for h in range(heads):
        u = pre[:, h * HEAD : (h + 1) * HEAD]
        q_ref[:, h * HEAD : (h + 1) * HEAD] = (turn(u, cosine, sine) * scale).astype(BF16)
    u = pre[:, heads * HEAD :]
    kv_ref[...] = jnp.where(core_ref[0] == 0, turn(u, cosine, sine), u).astype(BF16)


def qkv_half(core, x, first, cols, cosine, sine):
    rows, width = x.shape
    heads = cols // HEAD - 1
    tile = rows // 3
    return pl.pallas_call(
        functools.partial(qkv_kernel, heads),
        out_shape=(
            jax.ShapeDtypeStruct((rows, width), BF16),
            jax.ShapeDtypeStruct((rows, heads * HEAD), BF16),
            jax.ShapeDtypeStruct((rows, HEAD), BF16),
        ),
        grid=(rows // tile,),
        in_specs=[
            ANY_SMEM,
            pl.BlockSpec((tile, width), lambda r: (r, 0)),
            pl.BlockSpec((cols, width), lambda r: (0, 0)),
            pl.BlockSpec((16, width), lambda r: (cols // 16, 0)),
            pl.BlockSpec((tile, HEAD), lambda r: (r, 0)),
            pl.BlockSpec((tile, HEAD), lambda r: (r, 0)),
        ],
        out_specs=(
            pl.BlockSpec((tile, width), lambda r: (r, 0)),
            pl.BlockSpec((tile, heads * HEAD), lambda r: (r, 0)),
            pl.BlockSpec((tile, HEAD), lambda r: (r, 0)),
        ),
        cost_estimate=pl.CostEstimate(
            flops=2 * rows * width * cols, bytes_accessed=rows * width * 4 + cols * width * 2, transcendentals=0
        ),
        name="qkv",
    )(core, x, first, first, cosine, sine)


def to_order(starts_ref, mine, other, dest, block):
    per = mine.shape[0] // block
    for a in range(2 * per):
        src = mine if a < per else other
        at = pl.multiple_of(starts_ref[a], block)
        row = (a % per) * block
        for h in range(dest.shape[0]):
            dest[h, pl.ds(at, block), :] = src[row : row + block, h * HEAD : (h + 1) * HEAD]


def keys_in_order(starts_ref, own, got, k_n, v_n, block):
    @pl.when(starts_ref[16] == 0)
    def _():
        to_order(starts_ref, *own, k_n, block)
        to_order(starts_ref, *got, v_n, block)

    @pl.when(starts_ref[16] != 0)
    def _():
        to_order(starts_ref, *own, v_n, block)
        to_order(starts_ref, *got, k_n, block)


def over_queries(heads, seq, slot, step, visit):
    per = slot // step
    for first in range(0, seq, slot):

        def one(i, carry):
            visit(i // per, pl.multiple_of(first + lax.rem(i, per) * step, step), first + slot)
            return carry

        lax.fori_loop(0, heads * per, one, 0)


def attn_forward_kernel(
    slot, block, starts_ref, qm, qo, km, ko, rm, ro, lo_ref, hi_ref, om, oo, lse_ref, q_n, k_n, v_n, o_n, vt_n
):
    heads, seq, _ = q_n.shape
    to_order(starts_ref, qm, qo, q_n, block)
    keys_in_order(starts_ref, (km, ko), (rm, ro), k_n, v_n, block)
    vt_n[...] = v_n[0].astype(F32).T.astype(BF16)
    step = 256

    def visit(h, row, nk):
        rows = pl.ds(row, step)
        s = dot(k_n[0, :nk, :], q_n[h, rows, :], 1, 1)
        j = lax.broadcasted_iota(jnp.int32, s.shape, 0)
        ok = (j >= lo_ref[:, rows]) & (j <= hi_ref[:, rows])
        s = jnp.where(ok, s, -1e30)
        top = jnp.max(s, axis=0, keepdims=True)
        e = jnp.exp(s - top)
        total = jnp.sum(e, axis=0, keepdims=True)
        soft = (e * (1.0 / total)).astype(BF16)
        out = dot(vt_n[:, :nk], soft, 1, 0)
        o_n[h, rows, :] = out.T.astype(BF16)
        lse_ref[h, :, rows] = top + jnp.log(total)

    over_queries(heads, seq, slot, step, visit)
    per = om.shape[0] // block
    for a in range(2 * per):
        dest = om if a < per else oo
        row = (a % per) * block
        for h in range(heads):
            dest[row : row + block, h * HEAD : (h + 1) * HEAD] = o_n[
                h, pl.ds(pl.multiple_of(starts_ref[a], block), block), :
            ]


def attn_forward(starts, q, own, got, lo, hi, slot):
    half, q_cols = q[0].shape
    heads = q_cols // HEAD
    seq = 2 * half
    return pl.pallas_call(
        functools.partial(attn_forward_kernel, slot, seq // 16),
        out_shape=(
            jax.ShapeDtypeStruct((half, q_cols), BF16),
            jax.ShapeDtypeStruct((half, q_cols), BF16),
            jax.ShapeDtypeStruct((heads, 1, seq), F32),
        ),
        in_specs=[ANY_SMEM] + [ANY_VMEM] * 8,
        out_specs=(ANY_VMEM, ANY_VMEM, ANY_VMEM),
        scratch_shapes=[
            pltpu.VMEM((heads, seq, HEAD), BF16),
            pltpu.VMEM((1, seq, HEAD), BF16),
            pltpu.VMEM((1, seq, HEAD), BF16),
            pltpu.VMEM((heads, seq, HEAD), BF16),
            pltpu.VMEM((HEAD, seq), BF16),
        ],
        cost_estimate=pl.CostEstimate(
            flops=12 * seq * seq * q_cols, bytes_accessed=seq * q_cols * 8, transcendentals=heads * seq * seq
        ),
        name="attn_forward",
    )(starts, q[0], q[1], own[0], own[1], got[0], got[1], lo, hi)


def attn_backward_kernel(
    slot, block, starts_ref, qm, qo, km, ko, rm, ro, dom, doo, om, oo, lse_ref, lo_ref, hi_ref, cos_ref, sin_ref,
    dqm, dqo, keepm, keepo, sendm, sendo, q_n, k_n, v_n, do_n, o_n, kt_n, dq_n, dk_n, dv_n,
):
    heads, seq, _ = q_n.shape
    to_order(starts_ref, qm, qo, q_n, block)
    to_order(starts_ref, dom, doo, do_n, block)
    to_order(starts_ref, om, oo, o_n, block)
    keys_in_order(starts_ref, (km, ko), (rm, ro), k_n, v_n, block)
    kt_n[...] = k_n[0].astype(F32).T.astype(BF16)
    dk_n[...] = jnp.zeros_like(dk_n)
    dv_n[...] = jnp.zeros_like(dv_n)
    step = slot

    def visit(h, row, nk):
        rows = pl.ds(row, step)
        q = q_n[h, rows, :]
        d_out = do_n[h, rows, :]
        s = dot(k_n[0, :nk, :], q, 1, 1)
        j = lax.broadcasted_iota(jnp.int32, s.shape, 0)
        ok = (j >= lo_ref[:, rows]) & (j <= hi_ref[:, rows])
        soft = jnp.exp(jnp.where(ok, s - lse_ref[h, :, rows], -1e30))
        d_soft = dot(v_n[0, :nk, :], d_out, 1, 1)
        delta = jnp.sum((d_out.astype(F32) * o_n[h, rows, :].astype(F32)).T, axis=0, keepdims=True)
        d_s = (soft * (d_soft - delta)).astype(BF16)
        dv_n[:nk, :] += dot(soft.astype(BF16), d_out, 1, 0)
        dk_n[:nk, :] += dot(d_s, q, 1, 0)
        dq_n[h, rows, :] = dot(kt_n[:, :nk], d_s, 1, 0).T

    over_queries(heads, seq, slot, step, visit)
    per = dqm.shape[0] // block
    scale = 1.0 / math.sqrt(HEAD)
    first = starts_ref[16] == 0
    for a in range(2 * per):
        dq_to, keep_to, send_to = (dqm, keepm, sendm) if a < per else (dqo, keepo, sendo)
        row = (a % per) * block
        here = slice(row, row + block)
        there = pl.ds(pl.multiple_of(starts_ref[a], block), block)
        cosine, sine = cos_ref[a * block : (a + 1) * block, :], -sin_ref[a * block : (a + 1) * block, :]
        for h in range(heads):
            dq_to[here, h * HEAD : (h + 1) * HEAD] = (
                turn(dq_n[h, there, :], cosine, sine) * scale
            ).astype(BF16)
        dk = turn(dk_n[there, :], cosine, sine)
        dv = dv_n[there, :]
        keep_to[here, :] = jnp.where(first, dk, dv)
        send_to[here, :] = jnp.where(first, dv, dk).astype(BF16)


def attn_backward(starts, q, own, got, d_out, out, lse, lo, hi, cosine, sine, slot):
    half, q_cols = q[0].shape
    heads = q_cols // HEAD
    seq = 2 * half
    pair = lambda cols, dtype: [jax.ShapeDtypeStruct((half, cols), dtype)] * 2
    return pl.pallas_call(
        functools.partial(attn_backward_kernel, slot, seq // 16),
        out_shape=tuple(pair(q_cols, BF16) + pair(HEAD, F32) + pair(HEAD, BF16)),
        in_specs=[ANY_SMEM] + [ANY_VMEM] * 15,
        out_specs=(ANY_VMEM,) * 6,
        scratch_shapes=[
            pltpu.VMEM((heads, seq, HEAD), BF16),
            pltpu.VMEM((1, seq, HEAD), BF16),
            pltpu.VMEM((1, seq, HEAD), BF16),
            pltpu.VMEM((heads, seq, HEAD), BF16),
            pltpu.VMEM((heads, seq, HEAD), BF16),
            pltpu.VMEM((HEAD, seq), BF16),
            pltpu.VMEM((heads, seq, HEAD), F32),
            pltpu.VMEM((seq, HEAD), F32),
            pltpu.VMEM((seq, HEAD), F32),
        ],
        cost_estimate=pl.CostEstimate(
            flops=24 * seq * seq * q_cols, bytes_accessed=seq * q_cols * 16, transcendentals=heads * seq * seq
        ),
        name="attn_backward",
    )(starts, *q, *own, *got, *d_out, *out, lse, lo, hi, cosine, sine)


def hidden_kernel(ff, w_ref, n2_ref, df_ref, out_ref):
    dh = dot(w_ref[2 * ff :, :], df_ref[...], 1, 1)
    gu = dot(w_ref[: 2 * ff, :], n2_ref[...], 1, 1)
    gate, up = gu[:ff], gu[ff:]
    sig = jax.nn.sigmoid(gate)
    silu = gate * sig
    out_ref[:ff, :] = (dh * up * (sig * (1.0 + gate * (1.0 - sig)))).astype(BF16)
    out_ref[ff : 2 * ff, :] = (dh * silu).astype(BF16)
    out_ref[2 * ff :, :] = (silu * up).astype(BF16)


def hidden_half(w, n2, df):
    rows, width = n2.shape
    ff = w.shape[0] // 3
    tile = rows // 3
    return pl.pallas_call(
        functools.partial(hidden_kernel, ff),
        out_shape=jax.ShapeDtypeStruct((3 * ff, rows), BF16),
        grid=(rows // tile,),
        in_specs=[
            pl.BlockSpec((3 * ff, width), lambda r: (0, 0), pipeline_mode=pl.Buffered(1)),
            pl.BlockSpec((tile, width), lambda r: (r, 0)),
            pl.BlockSpec((tile, width), lambda r: (r, 0)),
        ],
        out_specs=pl.BlockSpec((3 * ff, tile), lambda r: (0, r)),
        cost_estimate=pl.CostEstimate(
            flops=6 * rows * width * ff, bytes_accessed=6 * ff * width, transcendentals=ff * rows
        ),
        name="hidden",
    )(w, n2, df)


def grads_kernel(ff, lm_ref, lo_ref, nm_ref, no_ref, dm_ref, do_ref, out_ref):
    out_ref[: 2 * ff, :] = (
        dot(lm_ref[: 2 * ff, :], nm_ref[...], 1, 0) + dot(lo_ref[: 2 * ff, :], no_ref[...], 1, 0)
    ).astype(BF16)
    out_ref[2 * ff :, :] = (
        dot(lm_ref[2 * ff :, :], dm_ref[...], 1, 0) + dot(lo_ref[2 * ff :, :], do_ref[...], 1, 0)
    ).astype(BF16)


def feed_grads(left, n2, df):
    rows, half = left[0].shape
    width = n2[0].shape[1]
    tile = 256
    whole = pl.BlockSpec((rows, half), lambda j: (0, 0), pipeline_mode=pl.Buffered(1))
    part = pl.BlockSpec((half, tile), lambda j: (0, j))
    return pl.pallas_call(
        functools.partial(grads_kernel, rows // 3),
        out_shape=jax.ShapeDtypeStruct((rows, width), BF16),
        grid=(width // tile,),
        in_specs=[whole, whole, part, part, part, part],
        out_specs=pl.BlockSpec((rows, tile), lambda j: (0, j)),
        cost_estimate=pl.CostEstimate(
            flops=4 * rows * half * width, bytes_accessed=rows * width * 2, transcendentals=0
        ),
        name="feed_grads",
    )(*left, *n2, *df)


def add_last_kernel(a0, b0, a1, b1, *rest):
    out, rows = rest[-1], b0.shape[0]
    out[:rows, :] = a0[:rows, :].astype(F32) + b0[...].astype(F32)
    out[rows:, :] = a1[:rows, :].astype(F32) + b1[...].astype(F32)


def collect_end_after(state, *others):
    one, two = state
    h, width = one.shape[0] // 2, one.shape[1]
    return pl.pallas_call(
        add_last_kernel,
        out_shape=jax.ShapeDtypeStruct((2 * h, width), F32),
        in_specs=[ANY_VMEM] * 4 + [pl.BlockSpec(memory_space=pl.ANY)] * len(others),
        out_specs=ANY_VMEM,
        name="add_last",
    )(one, side(one[h:]), two, far(two[h:]), *others)


def hold_kernel(v_ref, *rest):
    rest[-1][...] = v_ref[...]


def hold(v, *others):
    rows, width = v.shape
    tile = rows // 3 if rows % 48 == 0 else rows
    return pl.pallas_call(
        hold_kernel,
        out_shape=jax.ShapeDtypeStruct(v.shape, v.dtype),
        grid=(rows // tile,),
        in_specs=[pl.BlockSpec((tile, width), lambda i: (i, 0))] + [pl.BlockSpec(memory_space=pl.ANY)] * len(others),
        out_specs=pl.BlockSpec((tile, width), lambda i: (i, 0)),
        name="hold",
    )(v, *others)


def bring(c_ref, first, rows, refs, buf, sems):
    copies = [
        pltpu.make_async_copy(
            ref.at[pl.ds(start, rows), :], buf.at[lax.bitwise_xor(c_ref[0], bits)], sems.at[bits]
        )
        for bits, (ref, start) in enumerate(zip(refs, first))
    ]
    for copy in copies:
        copy.start()
    for copy in copies:
        copy.wait()


def finish_kernel(turned, sizes, c_ref, *refs):
    parts = len(sizes)
    pieces, out_ref, bufs, sems = refs[: 4 * parts], refs[4 * parts], refs[4 * parts + 1 : -1], refs[-1]
    for part, rows in enumerate(sizes):
        bring(c_ref, turned[1][part], rows, pieces[4 * part : 4 * part + 4], bufs[part], sems.at[part])
    at = 0
    for k in range(4):
        for part, rows in enumerate(sizes):
            v = bufs[part][k].astype(F32)
            if turned[0]:
                out_ref[:, at : at + rows] = v.T
            else:
                out_ref[at : at + rows, :] = v
            at += rows


def finish(c, sizes, turned, parts):
    width = parts[0][0][0].shape[1]
    total = 4 * sum(sizes)
    shape = (width, total) if turned else (total, width)
    firsts = [[first for _, first in part] for part in parts]
    return pl.pallas_call(
        functools.partial(finish_kernel, (turned, firsts), sizes),
        out_shape=jax.ShapeDtypeStruct(shape, F32),
        in_specs=[ANY_SMEM] + [pl.BlockSpec(memory_space=pl.ANY)] * (4 * len(parts)),
        out_specs=ANY_VMEM,
        scratch_shapes=[pltpu.VMEM((4, rows, width), BF16) for rows in sizes]
        + [pltpu.SemaphoreType.DMA((len(parts), 4))],
        name="finish",
    )(c, *[v for part in parts for v, _ in part])


def finish_attn_kernel(q_cols, c_ref, r0, r1, r2, r3, q_ref, k_ref, v_ref, o_ref, gain_ref, buf, sems):
    rows = buf.shape[1]
    bring(c_ref, (0,) * 4, rows, (r0, r1, r2, r3), buf, sems)
    qkv = q_cols + HEAD
    for k in range(4):
        q_ref[:, k * q_cols : (k + 1) * q_cols] = buf[k, :q_cols, :].astype(F32).T
        to = v_ref if k % 2 else k_ref
        to[:, (k // 2) * HEAD : (k // 2 + 1) * HEAD] = buf[k, q_cols:qkv, :].astype(F32).T
        o_ref[k * q_cols : (k + 1) * q_cols, :] = buf[k, qkv + 16 :, :].astype(F32)
    gain_ref[...] = sum(buf[k, qkv : qkv + 16, :].astype(F32) for k in range(4))


def finish_attn(c, q_cols, pieces):
    rows, width = pieces[0].shape
    shapes = [(width, 4 * q_cols), (width, 2 * HEAD), (width, 2 * HEAD), (4 * q_cols, width), (16, width)]
    return pl.pallas_call(
        functools.partial(finish_attn_kernel, q_cols),
        out_shape=tuple(jax.ShapeDtypeStruct(shape, F32) for shape in shapes),
        in_specs=[ANY_SMEM] + [pl.BlockSpec(memory_space=pl.ANY)] * 4,
        out_specs=(ANY_VMEM,) * 5,
        scratch_shapes=[pltpu.VMEM((4, rows, width), BF16), pltpu.SemaphoreType.DMA((4,))],
        name="finish_attn",
    )(c, *pieces)


def tables(c, t, core, tok_rows, seq_ids, pic_starts, pic_lengths):
    seq_len = seq_ids.shape[1]
    start_list = arrival_starts(c, t, tok_rows)
    starts = jnp.stack(start_list + [core]).astype(jnp.int32)
    positions = (starts[:16, None] + jnp.arange(seq_len // 16, dtype=jnp.int32)[None, :]).reshape(-1)
    frequency = jnp.power(rope_base, -jnp.arange(HEAD // 2, dtype=F32) * 2.0 / HEAD)
    angles = positions.astype(F32)[:, None] * frequency[None, :]
    cosine, sine = jnp.cos(angles), jnp.sin(angles)
    cosine = jnp.concatenate([cosine, cosine], axis=1)
    sine = jnp.concatenate([-sine, sine], axis=1)
    docs = seq_ids[0]
    index = jnp.arange(seq_len, dtype=jnp.int32)
    lo = jnp.sum((docs[:, None] < docs[None, :]).astype(jnp.int32), axis=0)
    doc_end = jnp.sum((docs[:, None] <= docs[None, :]).astype(jnp.int32), axis=0) - 1
    pic_ends = pic_starts[0] + pic_lengths[0]
    inside = (index[:, None] >= pic_starts[0][None, :]) & (index[:, None] < pic_ends[None, :])
    last = jnp.max(jnp.where(inside, pic_ends[None, :] - 1, -1), axis=1)
    hi = jnp.minimum(doc_end, jnp.maximum(index, last))
    lo, hi = lo[None, :], hi[None, :]
    return starts, cosine, sine, lo, hi


def body(
    tokens,
    seq_ids,
    pic_starts,
    pic_lengths,
    skip_mask,
    w_query,
    w_key,
    w_value,
    w_out,
    w_gate,
    w_up,
    w_down,
    gain_attn,
    gain_ffn,
    cotangent,
):
    tok_rows = tokens.shape[1]
    own = tok_rows // 2
    seq_len = seq_ids.shape[1]
    slot = seq_len // pic_starts.shape[1]
    c = lax.axis_index("ctx")
    t = lax.axis_index("tp")
    core = (c & 1).astype(jnp.int32)
    q_cols = w_query.shape[1] // 4
    ff = w_gate.shape[1] // 4
    part_a = (ff * 5 // 8 + 15) // 16 * 16
    part_b = ff - part_a

    flag = seq_ids[0, 0] >= 0
    qkv_cols = q_cols + HEAD
    half = seq_len // 2
    core_flag = core.reshape(1)
    first_own = pack_first(
        jnp.stack([c, core, c >> 1]).astype(jnp.int32), w_query, w_key, w_value, w_out, gain_attn, gain_ffn
    )
    first = gather_whole(first_own)

    def start_stage(tokens, skip_mask, cotangent, w_gate, w_up, w_down, seq_ids, pic_starts, pic_lengths):
        x_own_b = lax.dynamic_slice_in_dim(tokens[0], t * own, own, 0)
        keep_own = lax.dynamic_slice_in_dim(skip_mask[0], t * own, own, 0).astype(F32)[:, None]
        dy_own = lax.dynamic_slice_in_dim(cotangent[0], t * own, own, 0).astype(F32)
        parts = spread_start(x_own_b)
        wd_own = lax.dynamic_slice_in_dim(w_down, c * ff, ff, 0)
        wg_t = lax.dynamic_slice_in_dim(w_gate, c * ff, ff, 1).T
        wu_t = lax.dynamic_slice_in_dim(w_up, c * ff, ff, 1).T
        weights = [
            jnp.concatenate([v[first:last] for v in (wg_t, wu_t, wd_own)], axis=0)
            for first, last in ((0, part_a), (part_a, ff))
        ]
        parts = after(parts, weights)
        ready = parts[:2] + spread_more(parts)
        table = tables(c, t, core, tok_rows, seq_ids, pic_starts, pic_lengths)
        d_ffn_own = (keep_own * dy_own).astype(BF16)
        x_mine = spread_join(after(ready, table, d_ffn_own))
        x_other = near(x_mine)
        return x_own_b.astype(F32), keep_own, dy_own, d_ffn_own, x_mine, x_other, weights, table

    x_own, keep_own, dy_own, d_ffn_own, x_mine, x_other, weights, (starts, cosine, sine, lo, hi) = fenced(
        flag, start_stage,
        *after((tokens, skip_mask, cotangent, w_gate, w_up, w_down, seq_ids, pic_starts, pic_lengths), first_own)
    )
    weights = after(weights, x_other)
    wa, wb = gather_whole(weights[0]), gather_whole(weights[1])

    def forward_stage(x_mine, x_other, first, d_ffn_own, x_own, keep_own, cosine, sine, lo, hi, starts):
        wo = first[qkv_cols + 16 :]
        gain_two = first[qkv_cols + 1 : qkv_cols + 2].astype(F32)
        df_parts = spread_start(d_ffn_own)
        n1m, qm, kvm = qkv_half(core_flag, x_mine, first, qkv_cols, cosine[:half], sine[:half])
        n1o, qo, kvo = qkv_half(core_flag, x_other, first, qkv_cols, cosine[half:], sine[half:])
        q, own_kv = (qm, qo), (kvm, kvo)
        got = (near(kvo), near(kvm))
        q = after(q, df_parts)
        df_ready = df_parts[:2] + spread_more(df_parts)
        hm, ho, lse = attn_forward(starts, q, own_kv, got, lo, hi, slot)
        hm, ho = after((hm, ho), df_ready)
        both = join_cores(dot(hm, wo, 1, 0).astype(BF16), dot(ho, wo, 1, 0).astype(BF16))
        state = collect_first(both)
        dfm = spread_join(after(df_ready, both))
        attn = collect_end(collect_second(after(state, dfm)))
        dfo = near(dfm)
        mid = x_own + keep_own * attn
        inv_two = lax.rsqrt(jnp.mean(mid * mid, axis=-1, keepdims=True) + norm_eps)
        hat_two = mid * inv_two
        n2m, n2o = spread((hat_two * gain_two).astype(BF16))
        return n1m, n1o, q, own_kv, got, hm, ho, lse, dfm, dfo, n2m, n2o, mid, inv_two, hat_two

    n1m, n1o, q, own_kv, got, hm, ho, lse, dfm, dfo, n2m, n2o, mid, inv_two, hat_two = fenced(
        flag, forward_stage, x_mine, x_other, first, d_ffn_own, x_own, keep_own, cosine, sine, lo, hi, starts
    )

    am, ao = hidden_half(wa, n2m, dfm), hidden_half(wa, n2o, dfo)
    grad_a = feed_grads((am, ao), (n2m, n2o), (dfm, dfo))
    shard_a = scatter_whole(grad_a)
    pao = dot(ao[: 2 * part_a], wa[: 2 * part_a], 0, 0).astype(BF16)
    bm, bo = hidden_half(wb, n2m, dfm), hidden_half(wb, n2o, dfo)
    grad_b = feed_grads((bm, bo), (n2m, n2o), (dfm, dfo))
    shard_b = scatter_whole(grad_b)

    def middle_stage(am, ao, bm, bo, pao, wa, wb, first, dy_own, keep_own, hat_two, inv_two):
        gain_two = first[qkv_cols + 1 : qkv_cols + 2].astype(F32)
        p_other = (pao.astype(F32) + dot(bo[: 2 * part_b], wb[: 2 * part_b], 0, 0)).astype(BF16)
        p_mine = (
            dot(am[: 2 * part_a], wa[: 2 * part_a], 0, 0) + dot(bm[: 2 * part_b], wb[: 2 * part_b], 0, 0)
        ).astype(BF16)
        both = join_cores(p_mine, p_other)
        state = collect_first(both)
        am, ao, bm, bo = after((am, ao, bm, bo), both)

        def feed_out(a, b):
            return (
                dot(a[2 * part_a :], wa[2 * part_a :], 0, 0) + dot(b[2 * part_b :], wb[2 * part_b :], 0, 0)
            ).astype(BF16)

        f_other, f_mine = feed_out(ao, bo), feed_out(am, bm)
        d_n2 = collect_end(collect_second(after(state, f_other, f_mine)))
        d_mid = dy_own + norm_back(d_n2, hat_two, inv_two, gain_two)
        share_two = jnp.sum(d_n2 * hat_two, axis=0, keepdims=True)
        f_split = collect_split(join_cores(f_mine, f_other))
        dam, dao = spread((keep_own * d_mid).astype(BF16), f_split)
        d_head_m = dot(dam, first[qkv_cols + 16 :], 1, 1).astype(BF16)
        return d_mid, share_two, dam, dao, f_split, d_head_m

    bm, bo = after((bm, bo), grad_b)
    d_mid, share_two, dam, dao, f_split, d_head_m = fenced(
        flag, middle_stage, am, ao, bm, bo, pao, wa, wb, first, dy_own, keep_own, hat_two, inv_two
    )

    def backward_stage(
        share_two, dam, dao, f_split, d_head_m, first, q, own_kv, got, hm, ho, lse, lo, hi, cosine, sine, starts,
        x_mine, x_other, n1m, n1o, shard_a
    ):
        wqkv, wo = first[:qkv_cols], first[qkv_cols + 16 :]
        f_state = collect_send(f_split)
        d_head = (d_head_m, dot(dao, wo, 1, 1).astype(BF16))
        dqm, dqo, keepm, keepo, sendm, sendo = attn_backward(
            starts, q, own_kv, got, d_head, (hm, ho), lse, lo, hi, cosine, sine, slot
        )
        sendm, sendo = after((sendm, sendo), f_state)
        a_far = far(shard_a[: 2 * part_a])
        got_m, got_o = near(sendo), near(sendm)
        do = jnp.concatenate([dqo, (keepo + got_o.astype(F32)).astype(BF16)], axis=1)
        e_other = dot(do, wqkv, 1, 0).astype(BF16)
        dm = jnp.concatenate([dqm, (keepm + got_m.astype(F32)).astype(BF16)], axis=1)
        e_mine = dot(dm, wqkv, 1, 0).astype(BF16)
        both = join_cores(e_mine, e_other)
        state = collect_first(both)
        dm, do, hm, ho, x_mine, x_other = after((dm, do, hm, ho, x_mine, x_other), both)
        grad_qkv = (dot(dm, n1m, 0, 0) + dot(do, n1o, 0, 0)).astype(BF16)

        def gain_share(e, x):
            x = x.astype(F32)
            inv = lax.rsqrt(jnp.mean(x * x, axis=-1, keepdims=True) + norm_eps)
            return jnp.sum(e.astype(F32) * (x * inv), axis=0, keepdims=True)

        share_one = gain_share(e_mine, x_mine) + gain_share(e_other, x_other)
        shares = jnp.concatenate(
            [share_one, share_two, jnp.zeros((14, share_one.shape[1]), F32)], axis=0
        )
        shares_side = side(shares.astype(BF16))
        state = collect_second(after(state, grad_qkv, shares))
        hm, ho, dam, dao = after((hm, ho, dam, dao), state)
        grad_out = (dot(hm, dam, 0, 0) + dot(ho, dao, 0, 0)).astype(BF16)
        shares = (shares + shares_side.astype(F32)).astype(BF16)
        grad_attn = jnp.concatenate([grad_qkv, shares, grad_out], axis=0)
        d_n1 = collect_end_after(state, grad_out)
        return d_n1, grad_attn, collect_second(f_state), a_far

    d_n1, grad_attn, f_state, a_far = fenced(
        flag, backward_stage, share_two, dam, dao, f_split, d_head_m, first, q, own_kv, got, hm, ho, lse, lo, hi,
        cosine, sine, starts, x_mine, x_other, n1m, n1o, shard_a
    )
    shard_attn = scatter_whole(after(grad_attn, shard_b))
    member = c.astype(jnp.int32).reshape(1)

    def end_stage(d_n1, f_state, x_own, d_mid, first, mid, keep_own, shard_a, a_far, shard_b):
        gain_one = first[qkv_cols : qkv_cols + 1].astype(F32)
        ffn = collect_end(f_state)
        inv_one = lax.rsqrt(jnp.mean(x_own * x_own, axis=-1, keepdims=True) + norm_eps)
        hat_one = x_own * inv_one
        input_grad = (d_mid + norm_back(d_n1, hat_one, inv_one, gain_one)).astype(BF16)
        output = (mid + keep_own * ffn).astype(BF16)
        gate_far = far(hold(shard_b[:part_b], ffn))
        a_near, a_near_far, b_near = near(shard_a), near(a_far), near(shard_b)
        grad_gate = finish(
            member, sizes, True,
            [
                [(shard_a, 0), (a_near, 0), (a_far, 0), (a_near_far, 0)],
                [(shard_b, 0), (b_near, 0), (gate_far, 0), (near(gate_far), 0)],
            ],
        )
        rest = jnp.concatenate([shard_a[2 * part_a :], shard_b[part_b:]], axis=0)
        rest_far = hold(far(hold(rest, ffn)), grad_gate)
        return (
            in_order(input_grad, side(input_grad), t), output, grad_gate, a_near, a_near_far, b_near, rest_far, near(rest_far)
        )

    sizes = (part_a, part_b)
    input_grad, output, grad_gate, a_near, a_near_far, b_near, rest_far, near_far = fenced(
        flag, end_stage, d_n1, f_state, x_own, d_mid, first, mid, keep_own, shard_a, a_far, shard_b
    )

    def last_stage(shard_a, shard_b, a_near, a_far, a_near_far, b_near, rest_far, near_far, shard_attn, output):
        attn_far = far(shard_attn)
        up = [
            [(shard_a, part_a), (a_near, part_a), (a_far, part_a), (a_near_far, part_a)],
            [(shard_b, part_b), (b_near, part_b), (rest_far, part_a), (near_far, part_a)],
        ]
        down = [
            [(shard_a, 2 * part_a), (a_near, 2 * part_a), (rest_far, 0), (near_far, 0)],
            [(shard_b, 2 * part_b), (b_near, 2 * part_b), (rest_far, part_a + part_b), (near_far, part_a + part_b)],
        ]
        feed = finish(member, sizes, True, up), finish(member, sizes, False, down)
        attn_far = hold(attn_far, *feed)
        return feed, in_order(output, side(output), t), finish_attn(
            member, q_cols, (shard_attn, near(shard_attn), attn_far, near(attn_far))
        )

    (grad_up, grad_down), output, (grad_query, grad_key, grad_value, grad_out, gain_grads) = fenced(
        flag, last_stage, shard_a, shard_b, a_near, a_far, a_near_far, b_near, rest_far, near_far, shard_attn, output
    )
    return (
        output[None],
        input_grad[None],
        grad_query,
        grad_key,
        grad_value,
        grad_out,
        grad_gate,
        grad_up,
        grad_down,
        gain_grads[0],
        gain_grads[1],
    )


def solution(mesh):
    placed = (
        P("fsdp", "ctx", None),
        P("fsdp", None),
        P("fsdp", None),
        P("fsdp", None),
        P("fsdp", "ctx"),
        P("fsdp", "tp"),
        P("fsdp", "tp"),
        P("fsdp", "tp"),
        P("tp", "fsdp"),
        P("fsdp", "tp"),
        P("fsdp", "tp"),
        P("tp", "fsdp"),
        P("fsdp"),
        P("fsdp"),
        P("fsdp", "ctx", None),
    )
    return jax.shard_map(
        body,
        mesh=mesh,
        in_specs=placed,
        out_specs=(
            P("fsdp", "ctx", None),
            P("fsdp", "ctx", None),
            P("fsdp", "tp"),
            P("fsdp", "tp"),
            P("fsdp", "tp"),
            P("tp", "fsdp"),
            P("fsdp", "tp"),
            P("fsdp", "tp"),
            P("tp", "fsdp"),
            P("fsdp"),
            P("fsdp"),
        ),
        check_vma=False,
    )
```

```python
import functools
import math

import jax
import jax.numpy as jnp
from jax import lax
from jax.experimental import pallas as pl
from jax.experimental.pallas import tpu as pltpu
from jax.sharding import PartitionSpec as P

HEAD = 128
norm_eps = 1e-05
rope_base = 10000.0
F32 = jnp.float32
BF16 = jnp.bfloat16
ANY_VMEM = pl.BlockSpec(memory_space=pltpu.VMEM)
ANY_SMEM = pl.BlockSpec(memory_space=pltpu.SMEM)


def dot(a, b, ca, cb):
    return lax.dot_general(a, b, (((ca,), (cb,)), ((), ())), preferred_element_type=F32)


def after(v, *others):
    return lax.optimization_barrier((v,) + others)[0] if others else v


def fenced(flag, stage, *values):
    shapes = jax.eval_shape(stage, *values)

    def empty(*_):
        return jax.tree.map(lambda a: jnp.zeros(a.shape, a.dtype), shapes)

    return lax.cond(flag, stage, empty, *values)


def norm_back(d_normed, hat, inv_rms, gain):
    scaled = d_normed * gain
    return inv_rms * (scaled - hat * jnp.mean(scaled * hat, axis=-1, keepdims=True))


def far(v):
    return lax.ppermute(v, "ctx", [(i, i ^ 2) for i in range(4)])


def near(v):
    return lax.ppermute(v, "ctx", [(i, i ^ 1) for i in range(4)])


def side(v):
    return lax.ppermute(v, "tp", [(0, 1), (1, 0)])


def join_kernel(count, *refs):
    pieces, out_ref, sem = refs[:count], refs[-2], refs[-1]
    copies, row = [], 0
    for k, piece in enumerate(pieces):
        n = piece.shape[0]
        copies.append(pltpu.make_async_copy(piece, out_ref.at[pl.ds(row, n), :], sem.at[k]))
        copies[-1].start()
        row += n
    for copy in copies:
        copy.wait()


def join(*pieces, others=()):
    rows = sum(p.shape[0] for p in pieces)
    return pl.pallas_call(
        functools.partial(join_kernel, len(pieces)),
        out_shape=jax.ShapeDtypeStruct((rows, pieces[0].shape[1]), pieces[0].dtype),
        in_specs=[pl.BlockSpec(memory_space=pl.ANY)] * (len(pieces) + len(others)),
        out_specs=ANY_VMEM,
        scratch_shapes=[pltpu.SemaphoreType.DMA((len(pieces),))],
        name="join",
    )(*pieces, *others)


def spread_start(v):
    h = v.shape[0] // 2
    one, two = v[:h], v[h:]
    return one, two, far(one), side(two), side(one), far(two)


def spread_more(parts):
    one, two, one_far, two_side, one_side, two_far = parts
    return one_far, two_side, one_side, two_far, side(one_far), far(two_side)


def spread_join(ready, others=()):
    one, two, one_far, two_side, one_side, two_far, one_both, two_both = ready
    return join(one, one_far, one_side, one_both, two, two_side, two_far, two_both, others=others)


def spread(v, others=()):
    parts = spread_start(v)
    mine = spread_join(parts[:2] + spread_more(parts), others)
    return mine, near(mine)


def arrival_starts(c, t, tok_rows):
    own = tok_rows // 2
    starts = []
    for near_bit in range(2):
        for second in range(2):
            order = ((0, 0), (1, 0), (0, 1), (1, 1)) if second == 0 else ((0, 0), (0, 1), (1, 0), (1, 1))
            for far_bit, side_bit in order:
                ctx = c ^ (near_bit + 2 * far_bit)
                starts.append(ctx * tok_rows + (t ^ side_bit) * own + second * (own // 2))
    return starts


def collect_split(both):
    h = both.shape[0] // 8
    one = both[: 4 * h].reshape(2, 2, h, -1)
    two = both[4 * h :].reshape(2, 2, h, -1)
    return [v[:, k].reshape(2 * h, -1) for k in range(2) for v in (one, two)]


def collect_send(split):
    one, two, one_sent, two_sent = split
    return one, two, far(one_sent), side(two_sent)


def collect_first(both):
    return collect_send(collect_split(both))


def collect_second(state):
    one, two, one_far, two_side = state
    return add(one, one_far), add(two, two_side)


def collect_start(p_mine, p_other):
    return collect_second(collect_first(join_cores(p_mine, p_other)))


def join_cores(p_mine, p_other):
    return add(lax.optimization_barrier(p_mine), near(p_other))


def collect_end(state):
    one, two = state
    h = one.shape[0] // 2
    one_side = side(one[h:])
    two_far = far(two[h:])
    return jnp.concatenate(
        [
            one[:h].astype(F32) + one_side.astype(F32),
            two[:h].astype(F32) + two_far.astype(F32),
        ],
        axis=0,
    )


def collect(p_mine, p_other):
    return collect_end(collect_start(p_mine, p_other))


def in_order(v, other, t):
    return jnp.where(
        t == 0, jnp.concatenate([v, other], axis=0), jnp.concatenate([other, v], axis=0)
    )


def gather_whole(v):
    return lax.all_gather(v, "fsdp", axis=1, tiled=True)


def scatter_whole(g):
    return lax.psum_scatter(g, "fsdp", scatter_dimension=1, tiled=True)


def add(a, b):
    return (a.astype(F32) + b.astype(F32)).astype(BF16)


def pack_first_kernel(at_ref, wq_ref, wk_ref, wv_ref, wo_ref, one_ref, two_ref, out_ref):
    q_cols = wq_ref.shape[1]
    qkv = q_cols + HEAD
    out_ref[:q_cols, :] = wq_ref[...].astype(F32).T.astype(BF16)
    w_kv = jnp.where(at_ref[1] == 0, wk_ref[...].astype(F32), wv_ref[...].astype(F32))
    out_ref[q_cols:qkv, :] = w_kv.T.astype(BF16)
    row = lax.broadcasted_iota(jnp.int32, (16, out_ref.shape[1]), 0)
    one, two = one_ref[...].astype(F32)[None, :], two_ref[...].astype(F32)[None, :]
    out_ref[qkv : qkv + 16, :] = jnp.where(row == 0, one, jnp.where(row == 1, two, 0.0)).astype(BF16)
    out_ref[qkv + 16 :, :] = wo_ref[...]


def pack_first(at, w_query, w_key, w_value, w_out, gain_one, gain_two):
    depth = w_query.shape[0]
    q_cols = w_query.shape[1] // 4
    rows = 2 * q_cols + HEAD + 16
    gain = pl.BlockSpec((depth,), lambda i, at: (0,))
    return pl.pallas_call(
        pack_first_kernel,
        out_shape=jax.ShapeDtypeStruct((rows, depth), BF16),
        grid_spec=pltpu.PrefetchScalarGridSpec(
            num_scalar_prefetch=1,
            grid=(1,),
            in_specs=[
                pl.BlockSpec((depth, q_cols), lambda i, at: (0, at[0])),
                pl.BlockSpec((depth, HEAD), lambda i, at: (0, at[2])),
                pl.BlockSpec((depth, HEAD), lambda i, at: (0, at[2])),
                pl.BlockSpec((q_cols, depth), lambda i, at: (at[0], 0)),
                gain,
                gain,
            ],
            out_specs=pl.BlockSpec((rows, depth), lambda i, at: (0, 0)),
        ),
        name="pack_first",
    )(at, w_query, w_key, w_value, w_out, gain_one, gain_two)


def turn(u, cosine, sine):
    return u * cosine + pltpu.roll(u, HEAD // 2, 1) * sine


def qkv_kernel(heads, core_ref, x_ref, w_ref, gain_ref, cos_ref, sin_ref, n1_ref, q_ref, kv_ref):
    x = x_ref[...].astype(F32)
    inv = lax.rsqrt(jnp.mean(x * x, axis=-1, keepdims=True) + norm_eps)
    n1 = (x * inv * gain_ref[0:1, :].astype(F32)).astype(BF16)
    n1_ref[...] = n1
    pre = dot(n1, w_ref[...], 1, 1)
    cosine, sine = cos_ref[...], sin_ref[...]
    scale = 1.0 / math.sqrt(HEAD)
    for h in range(heads):
        u = pre[:, h * HEAD : (h + 1) * HEAD]
        q_ref[:, h * HEAD : (h + 1) * HEAD] = (turn(u, cosine, sine) * scale).astype(BF16)
    u = pre[:, heads * HEAD :]
    kv_ref[...] = jnp.where(core_ref[0] == 0, turn(u, cosine, sine), u).astype(BF16)


def qkv_half(core, x, first, cols, cosine, sine):
    rows, width = x.shape
    heads = cols // HEAD - 1
    tile = rows // 3
    return pl.pallas_call(
        functools.partial(qkv_kernel, heads),
        out_shape=(
            jax.ShapeDtypeStruct((rows, width), BF16),
            jax.ShapeDtypeStruct((rows, heads * HEAD), BF16),
            jax.ShapeDtypeStruct((rows, HEAD), BF16),
        ),
        grid=(rows // tile,),
        in_specs=[
            ANY_SMEM,
            pl.BlockSpec((tile, width), lambda r: (r, 0)),
            pl.BlockSpec((cols, width), lambda r: (0, 0)),
            pl.BlockSpec((16, width), lambda r: (cols // 16, 0)),
            pl.BlockSpec((tile, HEAD), lambda r: (r, 0)),
            pl.BlockSpec((tile, HEAD), lambda r: (r, 0)),
        ],
        out_specs=(
            pl.BlockSpec((tile, width), lambda r: (r, 0)),
            pl.BlockSpec((tile, heads * HEAD), lambda r: (r, 0)),
            pl.BlockSpec((tile, HEAD), lambda r: (r, 0)),
        ),
        cost_estimate=pl.CostEstimate(
            flops=2 * rows * width * cols, bytes_accessed=rows * width * 4 + cols * width * 2, transcendentals=0
        ),
        name="qkv",
    )(core, x, first, first, cosine, sine)


def to_order(starts_ref, mine, other, dest, block):
    per = mine.shape[0] // block
    for a in range(2 * per):
        src = mine if a < per else other
        at = pl.multiple_of(starts_ref[a], block)
        row = (a % per) * block
        for h in range(dest.shape[0]):
            dest[h, pl.ds(at, block), :] = src[row : row + block, h * HEAD : (h + 1) * HEAD]


def keys_in_order(starts_ref, own, got, k_n, v_n, block):
    @pl.when(starts_ref[16] == 0)
    def _():
        to_order(starts_ref, *own, k_n, block)
        to_order(starts_ref, *got, v_n, block)

    @pl.when(starts_ref[16] != 0)
    def _():
        to_order(starts_ref, *own, v_n, block)
        to_order(starts_ref, *got, k_n, block)


def over_queries(heads, seq, slot, step, visit, unrolled):
    def one(h, carry):
        for row in range(0, seq, step):
            visit(h, row, (row // slot + 1) * slot)
        return carry

    if unrolled:
        for h in range(heads):
            one(h, 0)
    else:
        lax.fori_loop(0, heads, one, 0)


def attn_forward_kernel(
    slot, block, starts_ref, qm, qo, km, ko, rm, ro, lo_ref, hi_ref, om, oo, lse_ref, q_n, k_n, v_n, o_n, vt_n
):
    heads, seq, _ = q_n.shape
    to_order(starts_ref, qm, qo, q_n, block)
    keys_in_order(starts_ref, (km, ko), (rm, ro), k_n, v_n, block)
    vt_n[...] = v_n[0].astype(F32).T.astype(BF16)
    step = 256

    def visit(h, row, nk):
        rows = pl.ds(row, step)
        s = dot(k_n[0, :nk, :], q_n[h, rows, :], 1, 1)
        j = lax.broadcasted_iota(jnp.int32, s.shape, 0)
        ok = (j >= lo_ref[:, rows]) & (j <= hi_ref[:, rows])
        s = jnp.where(ok, s, -1e30)
        top = jnp.max(s, axis=0, keepdims=True)
        e = jnp.exp(s - top)
        total = jnp.sum(e, axis=0, keepdims=True)
        soft = (e * (1.0 / total)).astype(BF16)
        out = dot(vt_n[:, :nk], soft, 1, 0)
        o_n[h, rows, :] = out.T.astype(BF16)
        lse_ref[h, :, rows] = top + jnp.log(total)

    over_queries(heads, seq, slot, step, visit, False)
    per = om.shape[0] // block
    for a in range(2 * per):
        dest = om if a < per else oo
        row = (a % per) * block
        for h in range(heads):
            dest[row : row + block, h * HEAD : (h + 1) * HEAD] = o_n[
                h, pl.ds(pl.multiple_of(starts_ref[a], block), block), :
            ]


def attn_forward(starts, q, own, got, lo, hi, slot):
    half, q_cols = q[0].shape
    heads = q_cols // HEAD
    seq = 2 * half
    return pl.pallas_call(
        functools.partial(attn_forward_kernel, slot, seq // 16),
        out_shape=(
            jax.ShapeDtypeStruct((half, q_cols), BF16),
            jax.ShapeDtypeStruct((half, q_cols), BF16),
            jax.ShapeDtypeStruct((heads, 1, seq), F32),
        ),
        in_specs=[ANY_SMEM] + [ANY_VMEM] * 8,
        out_specs=(ANY_VMEM, ANY_VMEM, ANY_VMEM),
        scratch_shapes=[
            pltpu.VMEM((heads, seq, HEAD), BF16),
            pltpu.VMEM((1, seq, HEAD), BF16),
            pltpu.VMEM((1, seq, HEAD), BF16),
            pltpu.VMEM((heads, seq, HEAD), BF16),
            pltpu.VMEM((HEAD, seq), BF16),
        ],
        cost_estimate=pl.CostEstimate(
            flops=12 * seq * seq * q_cols, bytes_accessed=seq * q_cols * 8, transcendentals=heads * seq * seq
        ),
        name="attn_forward",
    )(starts, q[0], q[1], own[0], own[1], got[0], got[1], lo, hi)


def attn_backward_kernel(
    slot, block, starts_ref, qm, qo, km, ko, rm, ro, dom, doo, om, oo, lse_ref, lo_ref, hi_ref, cos_ref, sin_ref,
    dqm, dqo, keepm, keepo, sendm, sendo, q_n, k_n, v_n, do_n, o_n, kt_n, dq_n, dk_n, dv_n,
):
    heads, seq, _ = q_n.shape
    to_order(starts_ref, qm, qo, q_n, block)
    to_order(starts_ref, dom, doo, do_n, block)
    to_order(starts_ref, om, oo, o_n, block)
    keys_in_order(starts_ref, (km, ko), (rm, ro), k_n, v_n, block)
    kt_n[...] = k_n[0].astype(F32).T.astype(BF16)
    dk_n[...] = jnp.zeros_like(dk_n)
    dv_n[...] = jnp.zeros_like(dv_n)
    step = slot

    def visit(h, row, nk):
        rows = pl.ds(row, step)
        q = q_n[h, rows, :]
        d_out = do_n[h, rows, :]
        s = dot(k_n[0, :nk, :], q, 1, 1)
        j = lax.broadcasted_iota(jnp.int32, s.shape, 0)
        ok = (j >= lo_ref[:, rows]) & (j <= hi_ref[:, rows])
        soft = jnp.exp(jnp.where(ok, s - lse_ref[h, :, rows], -1e30))
        d_soft = dot(v_n[0, :nk, :], d_out, 1, 1)
        delta = jnp.sum((d_out.astype(F32) * o_n[h, rows, :].astype(F32)).T, axis=0, keepdims=True)
        d_s = (soft * (d_soft - delta)).astype(BF16)
        dv_n[:nk, :] += dot(soft.astype(BF16), d_out, 1, 0)
        dk_n[:nk, :] += dot(d_s, q, 1, 0)
        dq_n[h, rows, :] = dot(kt_n[:, :nk], d_s, 1, 0).T

    over_queries(heads, seq, slot, step, visit, True)
    per = dqm.shape[0] // block
    scale = 1.0 / math.sqrt(HEAD)
    first = starts_ref[16] == 0
    for a in range(2 * per):
        dq_to, keep_to, send_to = (dqm, keepm, sendm) if a < per else (dqo, keepo, sendo)
        row = (a % per) * block
        here = slice(row, row + block)
        there = pl.ds(pl.multiple_of(starts_ref[a], block), block)
        cosine, sine = cos_ref[a * block : (a + 1) * block, :], -sin_ref[a * block : (a + 1) * block, :]
        for h in range(heads):
            dq_to[here, h * HEAD : (h + 1) * HEAD] = (
                turn(dq_n[h, there, :], cosine, sine) * scale
            ).astype(BF16)
        dk = turn(dk_n[there, :], cosine, sine)
        dv = dv_n[there, :]
        keep_to[here, :] = jnp.where(first, dk, dv)
        send_to[here, :] = jnp.where(first, dv, dk).astype(BF16)


def attn_backward(starts, q, own, got, d_out, out, lse, lo, hi, cosine, sine, slot):
    half, q_cols = q[0].shape
    heads = q_cols // HEAD
    seq = 2 * half
    pair = lambda cols, dtype: [jax.ShapeDtypeStruct((half, cols), dtype)] * 2
    return pl.pallas_call(
        functools.partial(attn_backward_kernel, slot, seq // 16),
        out_shape=tuple(pair(q_cols, BF16) + pair(HEAD, F32) + pair(HEAD, BF16)),
        in_specs=[ANY_SMEM] + [ANY_VMEM] * 15,
        out_specs=(ANY_VMEM,) * 6,
        scratch_shapes=[
            pltpu.VMEM((heads, seq, HEAD), BF16),
            pltpu.VMEM((1, seq, HEAD), BF16),
            pltpu.VMEM((1, seq, HEAD), BF16),
            pltpu.VMEM((heads, seq, HEAD), BF16),
            pltpu.VMEM((heads, seq, HEAD), BF16),
            pltpu.VMEM((HEAD, seq), BF16),
            pltpu.VMEM((heads, seq, HEAD), F32),
            pltpu.VMEM((seq, HEAD), F32),
            pltpu.VMEM((seq, HEAD), F32),
        ],
        cost_estimate=pl.CostEstimate(
            flops=24 * seq * seq * q_cols, bytes_accessed=seq * q_cols * 16, transcendentals=heads * seq * seq
        ),
        name="attn_backward",
    )(starts, *q, *own, *got, *d_out, *out, lse, lo, hi, cosine, sine)


def hidden_kernel(ff, w_ref, n2_ref, df_ref, out_ref):
    dh = dot(w_ref[2 * ff :, :], df_ref[...], 1, 1)
    gu = dot(w_ref[: 2 * ff, :], n2_ref[...], 1, 1)
    gate, up = gu[:ff], gu[ff:]
    sig = jax.nn.sigmoid(gate)
    silu = gate * sig
    out_ref[:ff, :] = (dh * up * (sig * (1.0 + gate * (1.0 - sig)))).astype(BF16)
    out_ref[ff : 2 * ff, :] = (dh * silu).astype(BF16)
    out_ref[2 * ff :, :] = (silu * up).astype(BF16)


def hidden_half(w, n2, df):
    rows, width = n2.shape
    ff = w.shape[0] // 3
    tile = rows // 3
    return pl.pallas_call(
        functools.partial(hidden_kernel, ff),
        out_shape=jax.ShapeDtypeStruct((3 * ff, rows), BF16),
        grid=(rows // tile,),
        in_specs=[
            pl.BlockSpec((3 * ff, width), lambda r: (0, 0), pipeline_mode=pl.Buffered(1)),
            pl.BlockSpec((tile, width), lambda r: (r, 0)),
            pl.BlockSpec((tile, width), lambda r: (r, 0)),
        ],
        out_specs=pl.BlockSpec((3 * ff, tile), lambda r: (0, r)),
        cost_estimate=pl.CostEstimate(
            flops=6 * rows * width * ff, bytes_accessed=6 * ff * width, transcendentals=ff * rows
        ),
        name="hidden",
    )(w, n2, df)


def grads_kernel(ff, lm_ref, lo_ref, nm_ref, no_ref, dm_ref, do_ref, out_ref):
    out_ref[: 2 * ff, :] = (
        dot(lm_ref[: 2 * ff, :], nm_ref[...], 1, 0) + dot(lo_ref[: 2 * ff, :], no_ref[...], 1, 0)
    ).astype(BF16)
    out_ref[2 * ff :, :] = (
        dot(lm_ref[2 * ff :, :], dm_ref[...], 1, 0) + dot(lo_ref[2 * ff :, :], do_ref[...], 1, 0)
    ).astype(BF16)


def feed_grads(left, n2, df):
    rows, half = left[0].shape
    width = n2[0].shape[1]
    tile = 256
    whole = pl.BlockSpec((rows, half), lambda j: (0, 0), pipeline_mode=pl.Buffered(1))
    part = pl.BlockSpec((half, tile), lambda j: (0, j))
    return pl.pallas_call(
        functools.partial(grads_kernel, rows // 3),
        out_shape=jax.ShapeDtypeStruct((rows, width), BF16),
        grid=(width // tile,),
        in_specs=[whole, whole, part, part, part, part],
        out_specs=pl.BlockSpec((rows, tile), lambda j: (0, j)),
        cost_estimate=pl.CostEstimate(
            flops=4 * rows * half * width, bytes_accessed=rows * width * 2, transcendentals=0
        ),
        name="feed_grads",
    )(*left, *n2, *df)


def add_last_kernel(a0, b0, a1, b1, *rest):
    out, rows = rest[-1], b0.shape[0]
    out[:rows, :] = a0[:rows, :].astype(F32) + b0[...].astype(F32)
    out[rows:, :] = a1[:rows, :].astype(F32) + b1[...].astype(F32)


def collect_end_after(state, *others):
    one, two = state
    h, width = one.shape[0] // 2, one.shape[1]
    return pl.pallas_call(
        add_last_kernel,
        out_shape=jax.ShapeDtypeStruct((2 * h, width), F32),
        in_specs=[ANY_VMEM] * 4 + [pl.BlockSpec(memory_space=pl.ANY)] * len(others),
        out_specs=ANY_VMEM,
        name="add_last",
    )(one, side(one[h:]), two, far(two[h:]), *others)


def hold_kernel(v_ref, *rest):
    rest[-1][...] = v_ref[...]


def hold(v, *others):
    rows, width = v.shape
    tile = rows // 3 if rows % 48 == 0 else rows
    return pl.pallas_call(
        hold_kernel,
        out_shape=jax.ShapeDtypeStruct(v.shape, v.dtype),
        grid=(rows // tile,),
        in_specs=[pl.BlockSpec((tile, width), lambda i: (i, 0))] + [pl.BlockSpec(memory_space=pl.ANY)] * len(others),
        out_specs=pl.BlockSpec((tile, width), lambda i: (i, 0)),
        name="hold",
    )(v, *others)


def bring(c_ref, first, rows, refs, buf, sems):
    copies = [
        pltpu.make_async_copy(
            ref.at[pl.ds(start, rows), :], buf.at[lax.bitwise_xor(c_ref[0], bits)], sems.at[bits]
        )
        for bits, (ref, start) in enumerate(zip(refs, first))
    ]
    for copy in copies:
        copy.start()
    for copy in copies:
        copy.wait()


def finish_kernel(turned, sizes, c_ref, *refs):
    parts = len(sizes)
    pieces, out_ref, bufs, sems = refs[: 4 * parts], refs[4 * parts], refs[4 * parts + 1 : -1], refs[-1]
    for part, rows in enumerate(sizes):
        bring(c_ref, turned[1][part], rows, pieces[4 * part : 4 * part + 4], bufs[part], sems.at[part])
    at = 0
    for k in range(4):
        for part, rows in enumerate(sizes):
            v = bufs[part][k].astype(F32)
            if turned[0]:
                out_ref[:, at : at + rows] = v.T
            else:
                out_ref[at : at + rows, :] = v
            at += rows


def finish(c, sizes, turned, parts):
    width = parts[0][0][0].shape[1]
    total = 4 * sum(sizes)
    shape = (width, total) if turned else (total, width)
    firsts = [[first for _, first in part] for part in parts]
    return pl.pallas_call(
        functools.partial(finish_kernel, (turned, firsts), sizes),
        out_shape=jax.ShapeDtypeStruct(shape, F32),
        in_specs=[ANY_SMEM] + [pl.BlockSpec(memory_space=pl.ANY)] * (4 * len(parts)),
        out_specs=ANY_VMEM,
        scratch_shapes=[pltpu.VMEM((4, rows, width), BF16) for rows in sizes]
        + [pltpu.SemaphoreType.DMA((len(parts), 4))],
        name="finish",
    )(c, *[v for part in parts for v, _ in part])


def finish_attn_kernel(q_cols, c_ref, r0, r1, r2, r3, q_ref, k_ref, v_ref, o_ref, gain_ref, buf, sems):
    rows = buf.shape[1]
    bring(c_ref, (0,) * 4, rows, (r0, r1, r2, r3), buf, sems)
    qkv = q_cols + HEAD
    for k in range(4):
        q_ref[:, k * q_cols : (k + 1) * q_cols] = buf[k, :q_cols, :].astype(F32).T
        to = v_ref if k % 2 else k_ref
        to[:, (k // 2) * HEAD : (k // 2 + 1) * HEAD] = buf[k, q_cols:qkv, :].astype(F32).T
        o_ref[k * q_cols : (k + 1) * q_cols, :] = buf[k, qkv + 16 :, :].astype(F32)
    gain_ref[...] = sum(buf[k, qkv : qkv + 16, :].astype(F32) for k in range(4))


def finish_attn(c, q_cols, pieces):
    rows, width = pieces[0].shape
    shapes = [(width, 4 * q_cols), (width, 2 * HEAD), (width, 2 * HEAD), (4 * q_cols, width), (16, width)]
    return pl.pallas_call(
        functools.partial(finish_attn_kernel, q_cols),
        out_shape=tuple(jax.ShapeDtypeStruct(shape, F32) for shape in shapes),
        in_specs=[ANY_SMEM] + [pl.BlockSpec(memory_space=pl.ANY)] * 4,
        out_specs=(ANY_VMEM,) * 5,
        scratch_shapes=[pltpu.VMEM((4, rows, width), BF16), pltpu.SemaphoreType.DMA((4,))],
        name="finish_attn",
    )(c, *pieces)


def tables(c, t, core, tok_rows, seq_ids, pic_starts, pic_lengths):
    seq_len = seq_ids.shape[1]
    start_list = arrival_starts(c, t, tok_rows)
    starts = jnp.stack(start_list + [core]).astype(jnp.int32)
    positions = (starts[:16, None] + jnp.arange(seq_len // 16, dtype=jnp.int32)[None, :]).reshape(-1)
    frequency = jnp.power(rope_base, -jnp.arange(HEAD // 2, dtype=F32) * 2.0 / HEAD)
    angles = positions.astype(F32)[:, None] * frequency[None, :]
    cosine, sine = jnp.cos(angles), jnp.sin(angles)
    cosine = jnp.concatenate([cosine, cosine], axis=1)
    sine = jnp.concatenate([-sine, sine], axis=1)
    docs = seq_ids[0]
    index = jnp.arange(seq_len, dtype=jnp.int32)
    lo = jnp.sum((docs[:, None] < docs[None, :]).astype(jnp.int32), axis=0)
    doc_end = jnp.sum((docs[:, None] <= docs[None, :]).astype(jnp.int32), axis=0) - 1
    pic_ends = pic_starts[0] + pic_lengths[0]
    inside = (index[:, None] >= pic_starts[0][None, :]) & (index[:, None] < pic_ends[None, :])
    last = jnp.max(jnp.where(inside, pic_ends[None, :] - 1, -1), axis=1)
    hi = jnp.minimum(doc_end, jnp.maximum(index, last))
    lo, hi = lo[None, :], hi[None, :]
    return starts, cosine, sine, lo, hi


def body(
    tokens,
    seq_ids,
    pic_starts,
    pic_lengths,
    skip_mask,
    w_query,
    w_key,
    w_value,
    w_out,
    w_gate,
    w_up,
    w_down,
    gain_attn,
    gain_ffn,
    cotangent,
):
    tok_rows = tokens.shape[1]
    own = tok_rows // 2
    seq_len = seq_ids.shape[1]
    slot = seq_len // pic_starts.shape[1]
    c = lax.axis_index("ctx")
    t = lax.axis_index("tp")
    core = (c & 1).astype(jnp.int32)
    q_cols = w_query.shape[1] // 4
    ff = w_gate.shape[1] // 4
    part_a = (ff * 3 // 4 + 15) // 16 * 16
    part_b = ff - part_a

    flag = seq_ids[0, 0] >= 0
    qkv_cols = q_cols + HEAD
    half = seq_len // 2
    core_flag = core.reshape(1)
    first_own = pack_first(
        jnp.stack([c, core, c >> 1]).astype(jnp.int32), w_query, w_key, w_value, w_out, gain_attn, gain_ffn
    )
    first = gather_whole(first_own)

    def start_stage(tokens, skip_mask, cotangent, w_gate, w_up, w_down, seq_ids, pic_starts, pic_lengths):
        x_own_b = lax.dynamic_slice_in_dim(tokens[0], t * own, own, 0)
        keep_own = lax.dynamic_slice_in_dim(skip_mask[0], t * own, own, 0).astype(F32)[:, None]
        dy_own = lax.dynamic_slice_in_dim(cotangent[0], t * own, own, 0).astype(F32)
        parts = spread_start(x_own_b)
        wd_own = lax.dynamic_slice_in_dim(w_down, c * ff, ff, 0)
        wg_t = lax.dynamic_slice_in_dim(w_gate, c * ff, ff, 1).T
        wu_t = lax.dynamic_slice_in_dim(w_up, c * ff, ff, 1).T
        weights = [
            jnp.concatenate([v[first:last] for v in (wg_t, wu_t, wd_own)], axis=0)
            for first, last in ((0, part_a), (part_a, ff))
        ]
        parts = after(parts, weights)
        ready = parts[:2] + spread_more(parts)
        table = tables(c, t, core, tok_rows, seq_ids, pic_starts, pic_lengths)
        d_ffn_own = (keep_own * dy_own).astype(BF16)
        x_mine = spread_join(after(ready, table, d_ffn_own))
        x_other = near(x_mine)
        return x_own_b.astype(F32), keep_own, dy_own, d_ffn_own, x_mine, x_other, weights, table

    x_own, keep_own, dy_own, d_ffn_own, x_mine, x_other, weights, (starts, cosine, sine, lo, hi) = fenced(
        flag, start_stage,
        *after((tokens, skip_mask, cotangent, w_gate, w_up, w_down, seq_ids, pic_starts, pic_lengths), first_own)
    )
    weights = after(weights, x_other)
    wa, wb = gather_whole(weights[0]), gather_whole(weights[1])

    def forward_stage(x_mine, x_other, first, d_ffn_own, x_own, keep_own, cosine, sine, lo, hi, starts):
        wo = first[qkv_cols + 16 :]
        gain_two = first[qkv_cols + 1 : qkv_cols + 2].astype(F32)
        df_parts = spread_start(d_ffn_own)
        n1m, qm, kvm = qkv_half(core_flag, x_mine, first, qkv_cols, cosine[:half], sine[:half])
        n1o, qo, kvo = qkv_half(core_flag, x_other, first, qkv_cols, cosine[half:], sine[half:])
        q, own_kv = (qm, qo), (kvm, kvo)
        got = (near(kvo), near(kvm))
        q = after(q, df_parts)
        df_ready = df_parts[:2] + spread_more(df_parts)
        hm, ho, lse = attn_forward(starts, q, own_kv, got, lo, hi, slot)
        hm, ho = after((hm, ho), df_ready)
        both = join_cores(dot(hm, wo, 1, 0).astype(BF16), dot(ho, wo, 1, 0).astype(BF16))
        state = collect_first(both)
        dfm = spread_join(after(df_ready, both))
        attn = collect_end(collect_second(after(state, dfm)))
        dfo = near(dfm)
        mid = x_own + keep_own * attn
        inv_two = lax.rsqrt(jnp.mean(mid * mid, axis=-1, keepdims=True) + norm_eps)
        hat_two = mid * inv_two
        n2m, n2o = spread((hat_two * gain_two).astype(BF16))
        return n1m, n1o, q, own_kv, got, hm, ho, lse, dfm, dfo, n2m, n2o, mid, inv_two, hat_two

    n1m, n1o, q, own_kv, got, hm, ho, lse, dfm, dfo, n2m, n2o, mid, inv_two, hat_two = fenced(
        flag, forward_stage, x_mine, x_other, first, d_ffn_own, x_own, keep_own, cosine, sine, lo, hi, starts
    )

    am, ao = hidden_half(wa, n2m, dfm), hidden_half(wa, n2o, dfo)
    grad_a = feed_grads((am, ao), (n2m, n2o), (dfm, dfo))
    shard_a = scatter_whole(grad_a)
    pao = dot(ao[: 2 * part_a], wa[: 2 * part_a], 0, 0).astype(BF16)
    bm, bo = hidden_half(wb, n2m, dfm), hidden_half(wb, n2o, dfo)
    grad_b = feed_grads((bm, bo), (n2m, n2o), (dfm, dfo))
    shard_b = scatter_whole(grad_b)

    def middle_stage(am, ao, bm, bo, pao, wa, wb, first, dy_own, keep_own, hat_two, inv_two):
        gain_two = first[qkv_cols + 1 : qkv_cols + 2].astype(F32)
        p_other = (pao.astype(F32) + dot(bo[: 2 * part_b], wb[: 2 * part_b], 0, 0)).astype(BF16)
        p_mine = (
            dot(am[: 2 * part_a], wa[: 2 * part_a], 0, 0) + dot(bm[: 2 * part_b], wb[: 2 * part_b], 0, 0)
        ).astype(BF16)
        both = join_cores(p_mine, p_other)
        state = collect_first(both)
        am, ao, bm, bo = after((am, ao, bm, bo), both)

        def feed_out(a, b):
            return (
                dot(a[2 * part_a :], wa[2 * part_a :], 0, 0) + dot(b[2 * part_b :], wb[2 * part_b :], 0, 0)
            ).astype(BF16)

        f_other, f_mine = feed_out(ao, bo), feed_out(am, bm)
        d_n2 = collect_end(collect_second(after(state, f_other, f_mine)))
        d_mid = dy_own + norm_back(d_n2, hat_two, inv_two, gain_two)
        share_two = jnp.sum(d_n2 * hat_two, axis=0, keepdims=True)
        f_split = collect_split(join_cores(f_mine, f_other))
        dam, dao = spread((keep_own * d_mid).astype(BF16), f_split)
        d_head_m = dot(dam, first[qkv_cols + 16 :], 1, 1).astype(BF16)
        return d_mid, share_two, dam, dao, f_split, d_head_m

    bm, bo = after((bm, bo), grad_b)
    d_mid, share_two, dam, dao, f_split, d_head_m = fenced(
        flag, middle_stage, am, ao, bm, bo, pao, wa, wb, first, dy_own, keep_own, hat_two, inv_two
    )

    def backward_stage(
        share_two, dam, dao, f_split, d_head_m, first, q, own_kv, got, hm, ho, lse, lo, hi, cosine, sine, starts,
        x_mine, x_other, n1m, n1o, shard_a
    ):
        wqkv, wo = first[:qkv_cols], first[qkv_cols + 16 :]
        f_state = collect_send(f_split)
        d_head = (d_head_m, dot(dao, wo, 1, 1).astype(BF16))
        dqm, dqo, keepm, keepo, sendm, sendo = attn_backward(
            starts, q, own_kv, got, d_head, (hm, ho), lse, lo, hi, cosine, sine, slot
        )
        sendm, sendo = after((sendm, sendo), f_state)
        a_far = far(shard_a[: 2 * part_a])
        got_m, got_o = near(sendo), near(sendm)
        do = jnp.concatenate([dqo, (keepo + got_o.astype(F32)).astype(BF16)], axis=1)
        e_other = dot(do, wqkv, 1, 0).astype(BF16)
        dm = jnp.concatenate([dqm, (keepm + got_m.astype(F32)).astype(BF16)], axis=1)
        e_mine = dot(dm, wqkv, 1, 0).astype(BF16)
        both = join_cores(e_mine, e_other)
        state = collect_first(both)
        dm, do, hm, ho, x_mine, x_other = after((dm, do, hm, ho, x_mine, x_other), both)
        grad_qkv = (dot(dm, n1m, 0, 0) + dot(do, n1o, 0, 0)).astype(BF16)

        def gain_share(e, x):
            x = x.astype(F32)
            inv = lax.rsqrt(jnp.mean(x * x, axis=-1, keepdims=True) + norm_eps)
            return jnp.sum(e.astype(F32) * (x * inv), axis=0, keepdims=True)

        share_one = gain_share(e_mine, x_mine) + gain_share(e_other, x_other)
        shares = jnp.concatenate(
            [share_one, share_two, jnp.zeros((14, share_one.shape[1]), F32)], axis=0
        )
        shares_side = side(shares.astype(BF16))
        state = collect_second(after(state, grad_qkv, shares))
        hm, ho, dam, dao = after((hm, ho, dam, dao), state)
        grad_out = (dot(hm, dam, 0, 0) + dot(ho, dao, 0, 0)).astype(BF16)
        shares = (shares + shares_side.astype(F32)).astype(BF16)
        grad_attn = jnp.concatenate([grad_qkv, shares, grad_out], axis=0)
        d_n1 = collect_end_after(state, grad_out)
        return d_n1, grad_attn, collect_second(f_state), a_far

    d_n1, grad_attn, f_state, a_far = fenced(
        flag, backward_stage, share_two, dam, dao, f_split, d_head_m, first, q, own_kv, got, hm, ho, lse, lo, hi,
        cosine, sine, starts, x_mine, x_other, n1m, n1o, shard_a
    )
    shard_attn = scatter_whole(after(grad_attn, shard_b))
    member = c.astype(jnp.int32).reshape(1)

    def end_stage(d_n1, f_state, x_own, d_mid, first, mid, keep_own, shard_a, a_far, shard_b):
        gain_one = first[qkv_cols : qkv_cols + 1].astype(F32)
        ffn = collect_end(f_state)
        inv_one = lax.rsqrt(jnp.mean(x_own * x_own, axis=-1, keepdims=True) + norm_eps)
        hat_one = x_own * inv_one
        input_grad = (d_mid + norm_back(d_n1, hat_one, inv_one, gain_one)).astype(BF16)
        output = (mid + keep_own * ffn).astype(BF16)
        gate_far = far(hold(shard_b[:part_b], ffn))
        a_near, a_near_far, b_near = near(shard_a), near(a_far), near(shard_b)
        grad_gate = finish(
            member, sizes, True,
            [
                [(shard_a, 0), (a_near, 0), (a_far, 0), (a_near_far, 0)],
                [(shard_b, 0), (b_near, 0), (gate_far, 0), (near(gate_far), 0)],
            ],
        )
        rest = jnp.concatenate([shard_a[2 * part_a :], shard_b[part_b:]], axis=0)
        rest_far = hold(far(hold(rest, ffn)), grad_gate)
        return (
            in_order(input_grad, side(input_grad), t), output, grad_gate, a_near, a_near_far, b_near, rest_far, near(rest_far)
        )

    sizes = (part_a, part_b)
    input_grad, output, grad_gate, a_near, a_near_far, b_near, rest_far, near_far = fenced(
        flag, end_stage, d_n1, f_state, x_own, d_mid, first, mid, keep_own, shard_a, a_far, shard_b
    )

    def last_stage(shard_a, shard_b, a_near, a_far, a_near_far, b_near, rest_far, near_far, shard_attn, output):
        attn_far = far(shard_attn)
        up = [
            [(shard_a, part_a), (a_near, part_a), (a_far, part_a), (a_near_far, part_a)],
            [(shard_b, part_b), (b_near, part_b), (rest_far, part_a), (near_far, part_a)],
        ]
        down = [
            [(shard_a, 2 * part_a), (a_near, 2 * part_a), (rest_far, 0), (near_far, 0)],
            [(shard_b, 2 * part_b), (b_near, 2 * part_b), (rest_far, part_a + part_b), (near_far, part_a + part_b)],
        ]
        feed = finish(member, sizes, True, up), finish(member, sizes, False, down)
        attn_far = hold(attn_far, *feed)
        return feed, in_order(output, side(output), t), finish_attn(
            member, q_cols, (shard_attn, near(shard_attn), attn_far, near(attn_far))
        )

    (grad_up, grad_down), output, (grad_query, grad_key, grad_value, grad_out, gain_grads) = fenced(
        flag, last_stage, shard_a, shard_b, a_near, a_far, a_near_far, b_near, rest_far, near_far, shard_attn, output
    )
    return (
        output[None],
        input_grad[None],
        grad_query,
        grad_key,
        grad_value,
        grad_out,
        grad_gate,
        grad_up,
        grad_down,
        gain_grads[0],
        gain_grads[1],
    )


def solution(mesh):
    placed = (
        P("fsdp", "ctx", None),
        P("fsdp", None),
        P("fsdp", None),
        P("fsdp", None),
        P("fsdp", "ctx"),
        P("fsdp", "tp"),
        P("fsdp", "tp"),
        P("fsdp", "tp"),
        P("tp", "fsdp"),
        P("fsdp", "tp"),
        P("fsdp", "tp"),
        P("tp", "fsdp"),
        P("fsdp"),
        P("fsdp"),
        P("fsdp", "ctx", None),
    )
    return jax.shard_map(
        body,
        mesh=mesh,
        in_specs=placed,
        out_specs=(
            P("fsdp", "ctx", None),
            P("fsdp", "ctx", None),
            P("fsdp", "tp"),
            P("fsdp", "tp"),
            P("fsdp", "tp"),
            P("tp", "fsdp"),
            P("fsdp", "tp"),
            P("fsdp", "tp"),
            P("tp", "fsdp"),
            P("fsdp"),
            P("fsdp"),
        ),
        check_vma=False,
    )
```

```python
import functools
import math

import jax
import jax.numpy as jnp
from jax import lax
from jax.experimental import pallas as pl
from jax.experimental.pallas import tpu as pltpu
from jax.sharding import PartitionSpec as P

HEAD = 128
norm_eps = 1e-05
rope_base = 10000.0
F32 = jnp.float32
BF16 = jnp.bfloat16
ANY_VMEM = pl.BlockSpec(memory_space=pltpu.VMEM)
ANY_SMEM = pl.BlockSpec(memory_space=pltpu.SMEM)


def dot(a, b, ca, cb):
    return lax.dot_general(a, b, (((ca,), (cb,)), ((), ())), preferred_element_type=F32)


def after(v, *others):
    return lax.optimization_barrier((v,) + others)[0] if others else v


def fenced(flag, stage, *values):
    shapes = jax.eval_shape(stage, *values)

    def empty(*_):
        return jax.tree.map(lambda a: jnp.zeros(a.shape, a.dtype), shapes)

    return lax.cond(flag, stage, empty, *values)


def norm_back(d_normed, hat, inv_rms, gain):
    scaled = d_normed * gain
    return inv_rms * (scaled - hat * jnp.mean(scaled * hat, axis=-1, keepdims=True))


def far(v):
    return lax.ppermute(v, "ctx", [(i, i ^ 2) for i in range(4)])


def near(v):
    return lax.ppermute(v, "ctx", [(i, i ^ 1) for i in range(4)])


def side(v):
    return lax.ppermute(v, "tp", [(0, 1), (1, 0)])


def join_kernel(count, *refs):
    pieces, out_ref, sem = refs[:count], refs[-2], refs[-1]
    copies, row = [], 0
    for k, piece in enumerate(pieces):
        n = piece.shape[0]
        copies.append(pltpu.make_async_copy(piece, out_ref.at[pl.ds(row, n), :], sem.at[k]))
        copies[-1].start()
        row += n
    for copy in copies:
        copy.wait()


def join(*pieces, others=()):
    rows = sum(p.shape[0] for p in pieces)
    return pl.pallas_call(
        functools.partial(join_kernel, len(pieces)),
        out_shape=jax.ShapeDtypeStruct((rows, pieces[0].shape[1]), pieces[0].dtype),
        in_specs=[pl.BlockSpec(memory_space=pl.ANY)] * (len(pieces) + len(others)),
        out_specs=ANY_VMEM,
        scratch_shapes=[pltpu.SemaphoreType.DMA((len(pieces),))],
        name="join",
    )(*pieces, *others)


def spread_start(v):
    h = v.shape[0] // 2
    one, two = v[:h], v[h:]
    return one, two, far(one), side(two), side(one), far(two)


def spread_more(parts):
    one, two, one_far, two_side, one_side, two_far = parts
    return one_far, two_side, one_side, two_far, side(one_far), far(two_side)


def spread_join(ready, others=()):
    one, two, one_far, two_side, one_side, two_far, one_both, two_both = ready
    return join(one, one_far, one_side, one_both, two, two_side, two_far, two_both, others=others)


def spread(v, others=()):
    parts = spread_start(v)
    mine = spread_join(parts[:2] + spread_more(parts), others)
    return mine, near(mine)


def arrival_starts(c, t, tok_rows):
    own = tok_rows // 2
    starts = []
    for near_bit in range(2):
        for second in range(2):
            order = ((0, 0), (1, 0), (0, 1), (1, 1)) if second == 0 else ((0, 0), (0, 1), (1, 0), (1, 1))
            for far_bit, side_bit in order:
                ctx = c ^ (near_bit + 2 * far_bit)
                starts.append(ctx * tok_rows + (t ^ side_bit) * own + second * (own // 2))
    return starts


def collect_split(both):
    h = both.shape[0] // 8
    one = both[: 4 * h].reshape(2, 2, h, -1)
    two = both[4 * h :].reshape(2, 2, h, -1)
    return [v[:, k].reshape(2 * h, -1) for k in range(2) for v in (one, two)]


def collect_send(split):
    one, two, one_sent, two_sent = split
    return one, two, far(one_sent), side(two_sent)


def collect_first(both):
    return collect_send(collect_split(both))


def collect_second(state):
    one, two, one_far, two_side = state
    return add(one, one_far), add(two, two_side)


def collect_start(p_mine, p_other):
    return collect_second(collect_first(join_cores(p_mine, p_other)))


def join_cores(p_mine, p_other):
    return add(lax.optimization_barrier(p_mine), near(p_other))


def collect_end(state):
    one, two = state
    h = one.shape[0] // 2
    one_side = side(one[h:])
    two_far = far(two[h:])
    return jnp.concatenate(
        [
            one[:h].astype(F32) + one_side.astype(F32),
            two[:h].astype(F32) + two_far.astype(F32),
        ],
        axis=0,
    )


def collect(p_mine, p_other):
    return collect_end(collect_start(p_mine, p_other))


def in_order(v, other, t):
    return jnp.where(
        t == 0, jnp.concatenate([v, other], axis=0), jnp.concatenate([other, v], axis=0)
    )


def gather_whole(v):
    return lax.all_gather(v, "fsdp", axis=1, tiled=True)


def scatter_whole(g):
    return lax.psum_scatter(g, "fsdp", scatter_dimension=1, tiled=True)


def add(a, b):
    return (a.astype(F32) + b.astype(F32)).astype(BF16)


def pack_first_kernel(at_ref, wq_ref, wk_ref, wv_ref, wo_ref, one_ref, two_ref, out_ref):
    q_cols = wq_ref.shape[1]
    qkv = q_cols + HEAD
    out_ref[:q_cols, :] = wq_ref[...].astype(F32).T.astype(BF16)
    w_kv = jnp.where(at_ref[1] == 0, wk_ref[...].astype(F32), wv_ref[...].astype(F32))
    out_ref[q_cols:qkv, :] = w_kv.T.astype(BF16)
    row = lax.broadcasted_iota(jnp.int32, (16, out_ref.shape[1]), 0)
    one, two = one_ref[...].astype(F32)[None, :], two_ref[...].astype(F32)[None, :]
    out_ref[qkv : qkv + 16, :] = jnp.where(row == 0, one, jnp.where(row == 1, two, 0.0)).astype(BF16)
    out_ref[qkv + 16 :, :] = wo_ref[...]


def pack_first(at, w_query, w_key, w_value, w_out, gain_one, gain_two):
    depth = w_query.shape[0]
    q_cols = w_query.shape[1] // 4
    rows = 2 * q_cols + HEAD + 16
    gain = pl.BlockSpec((depth,), lambda i, at: (0,))
    return pl.pallas_call(
        pack_first_kernel,
        out_shape=jax.ShapeDtypeStruct((rows, depth), BF16),
        grid_spec=pltpu.PrefetchScalarGridSpec(
            num_scalar_prefetch=1,
            grid=(1,),
            in_specs=[
                pl.BlockSpec((depth, q_cols), lambda i, at: (0, at[0])),
                pl.BlockSpec((depth, HEAD), lambda i, at: (0, at[2])),
                pl.BlockSpec((depth, HEAD), lambda i, at: (0, at[2])),
                pl.BlockSpec((q_cols, depth), lambda i, at: (at[0], 0)),
                gain,
                gain,
            ],
            out_specs=pl.BlockSpec((rows, depth), lambda i, at: (0, 0)),
        ),
        name="pack_first",
    )(at, w_query, w_key, w_value, w_out, gain_one, gain_two)


def turn(u, cosine, sine):
    return u * cosine + pltpu.roll(u, HEAD // 2, 1) * sine


def qkv_kernel(heads, core_ref, x_ref, w_ref, gain_ref, cos_ref, sin_ref, n1_ref, q_ref, kv_ref):
    x = x_ref[...].astype(F32)
    inv = lax.rsqrt(jnp.mean(x * x, axis=-1, keepdims=True) + norm_eps)
    n1 = (x * inv * gain_ref[0:1, :].astype(F32)).astype(BF16)
    n1_ref[...] = n1
    pre = dot(n1, w_ref[...], 1, 1)
    cosine, sine = cos_ref[...], sin_ref[...]
    scale = 1.0 / math.sqrt(HEAD)
    for h in range(heads):
        u = pre[:, h * HEAD : (h + 1) * HEAD]
        q_ref[:, h * HEAD : (h + 1) * HEAD] = (turn(u, cosine, sine) * scale).astype(BF16)
    u = pre[:, heads * HEAD :]
    kv_ref[...] = jnp.where(core_ref[0] == 0, turn(u, cosine, sine), u).astype(BF16)


def qkv_half(core, x, first, cols, cosine, sine):
    rows, width = x.shape
    heads = cols // HEAD - 1
    tile = rows // 3
    return pl.pallas_call(
        functools.partial(qkv_kernel, heads),
        out_shape=(
            jax.ShapeDtypeStruct((rows, width), BF16),
            jax.ShapeDtypeStruct((rows, heads * HEAD), BF16),
            jax.ShapeDtypeStruct((rows, HEAD), BF16),
        ),
        grid=(rows // tile,),
        in_specs=[
            ANY_SMEM,
            pl.BlockSpec((tile, width), lambda r: (r, 0)),
            pl.BlockSpec((cols, width), lambda r: (0, 0)),
            pl.BlockSpec((16, width), lambda r: (cols // 16, 0)),
            pl.BlockSpec((tile, HEAD), lambda r: (r, 0)),
            pl.BlockSpec((tile, HEAD), lambda r: (r, 0)),
        ],
        out_specs=(
            pl.BlockSpec((tile, width), lambda r: (r, 0)),
            pl.BlockSpec((tile, heads * HEAD), lambda r: (r, 0)),
            pl.BlockSpec((tile, HEAD), lambda r: (r, 0)),
        ),
        cost_estimate=pl.CostEstimate(
            flops=2 * rows * width * cols, bytes_accessed=rows * width * 4 + cols * width * 2, transcendentals=0
        ),
        name="qkv",
    )(core, x, first, first, cosine, sine)


def to_order(starts_ref, mine, other, dest, block):
    per = mine.shape[0] // block
    for a in range(2 * per):
        src = mine if a < per else other
        at = pl.multiple_of(starts_ref[a], block)
        row = (a % per) * block
        for h in range(dest.shape[0]):
            dest[h, pl.ds(at, block), :] = src[row : row + block, h * HEAD : (h + 1) * HEAD]


def keys_in_order(starts_ref, own, got, k_n, v_n, block):
    @pl.when(starts_ref[16] == 0)
    def _():
        to_order(starts_ref, *own, k_n, block)
        to_order(starts_ref, *got, v_n, block)

    @pl.when(starts_ref[16] != 0)
    def _():
        to_order(starts_ref, *own, v_n, block)
        to_order(starts_ref, *got, k_n, block)


def over_queries(heads, seq, slot, step, visit, unrolled):
    def one(h, carry):
        for row in range(0, seq, step):
            visit(h, row, (row // slot + 1) * slot)
        return carry

    if unrolled:
        for h in range(heads):
            one(h, 0)
    else:
        lax.fori_loop(0, heads, one, 0)


def attn_forward_kernel(
    slot, block, starts_ref, qm, qo, km, ko, rm, ro, lo_ref, hi_ref, om, oo, lse_ref, q_n, k_n, v_n, o_n, vt_n
):
    heads, seq, _ = q_n.shape
    to_order(starts_ref, qm, qo, q_n, block)
    keys_in_order(starts_ref, (km, ko), (rm, ro), k_n, v_n, block)
    vt_n[...] = v_n[0].astype(F32).T.astype(BF16)
    step = 256

    def visit(h, row, nk):
        rows = pl.ds(row, step)
        s = dot(k_n[0, :nk, :], q_n[h, rows, :], 1, 1)
        j = lax.broadcasted_iota(jnp.int32, s.shape, 0)
        ok = (j >= lo_ref[:, rows]) & (j <= hi_ref[:, rows])
        s = jnp.where(ok, s, -1e30)
        top = jnp.max(s, axis=0, keepdims=True)
        e = jnp.exp(s - top)
        total = jnp.sum(e, axis=0, keepdims=True)
        soft = (e * (1.0 / total)).astype(BF16)
        out = dot(vt_n[:, :nk], soft, 1, 0)
        o_n[h, rows, :] = out.T.astype(BF16)
        lse_ref[h, :, rows] = top + jnp.log(total)

    over_queries(heads, seq, slot, step, visit, False)
    per = om.shape[0] // block
    for a in range(2 * per):
        dest = om if a < per else oo
        row = (a % per) * block
        for h in range(heads):
            dest[row : row + block, h * HEAD : (h + 1) * HEAD] = o_n[
                h, pl.ds(pl.multiple_of(starts_ref[a], block), block), :
            ]


def attn_forward(starts, q, own, got, lo, hi, slot):
    half, q_cols = q[0].shape
    heads = q_cols // HEAD
    seq = 2 * half
    return pl.pallas_call(
        functools.partial(attn_forward_kernel, slot, seq // 16),
        out_shape=(
            jax.ShapeDtypeStruct((half, q_cols), BF16),
            jax.ShapeDtypeStruct((half, q_cols), BF16),
            jax.ShapeDtypeStruct((heads, 1, seq), F32),
        ),
        in_specs=[ANY_SMEM] + [ANY_VMEM] * 8,
        out_specs=(ANY_VMEM, ANY_VMEM, ANY_VMEM),
        scratch_shapes=[
            pltpu.VMEM((heads, seq, HEAD), BF16),
            pltpu.VMEM((1, seq, HEAD), BF16),
            pltpu.VMEM((1, seq, HEAD), BF16),
            pltpu.VMEM((heads, seq, HEAD), BF16),
            pltpu.VMEM((HEAD, seq), BF16),
        ],
        cost_estimate=pl.CostEstimate(
            flops=12 * seq * seq * q_cols, bytes_accessed=seq * q_cols * 8, transcendentals=heads * seq * seq
        ),
        name="attn_forward",
    )(starts, q[0], q[1], own[0], own[1], got[0], got[1], lo, hi)


def attn_backward_kernel(
    slot, block, starts_ref, qm, qo, km, ko, rm, ro, dom, doo, om, oo, lse_ref, lo_ref, hi_ref, cos_ref, sin_ref,
    dqm, dqo, keepm, keepo, sendm, sendo, q_n, k_n, v_n, do_n, o_n, kt_n, dq_n, dk_n, dv_n,
):
    heads, seq, _ = q_n.shape
    to_order(starts_ref, qm, qo, q_n, block)
    to_order(starts_ref, dom, doo, do_n, block)
    to_order(starts_ref, om, oo, o_n, block)
    keys_in_order(starts_ref, (km, ko), (rm, ro), k_n, v_n, block)
    kt_n[...] = k_n[0].astype(F32).T.astype(BF16)
    dk_n[...] = jnp.zeros_like(dk_n)
    dv_n[...] = jnp.zeros_like(dv_n)
    step = slot

    def visit(h, row, nk):
        rows = pl.ds(row, step)
        q = q_n[h, rows, :]
        d_out = do_n[h, rows, :]
        s = dot(k_n[0, :nk, :], q, 1, 1)
        j = lax.broadcasted_iota(jnp.int32, s.shape, 0)
        ok = (j >= lo_ref[:, rows]) & (j <= hi_ref[:, rows])
        soft = jnp.exp(jnp.where(ok, s - lse_ref[h, :, rows], -1e30))
        d_soft = dot(v_n[0, :nk, :], d_out, 1, 1)
        delta = jnp.sum((d_out.astype(F32) * o_n[h, rows, :].astype(F32)).T, axis=0, keepdims=True)
        d_s = (soft * (d_soft - delta)).astype(BF16)
        dv_n[:nk, :] += dot(soft.astype(BF16), d_out, 1, 0)
        dk_n[:nk, :] += dot(d_s, q, 1, 0)
        dq_n[h, rows, :] = dot(kt_n[:, :nk], d_s, 1, 0).T

    over_queries(heads, seq, slot, step, visit, True)
    per = dqm.shape[0] // block
    scale = 1.0 / math.sqrt(HEAD)
    first = starts_ref[16] == 0
    for a in range(2 * per):
        dq_to, keep_to, send_to = (dqm, keepm, sendm) if a < per else (dqo, keepo, sendo)
        row = (a % per) * block
        here = slice(row, row + block)
        there = pl.ds(pl.multiple_of(starts_ref[a], block), block)
        cosine, sine = cos_ref[a * block : (a + 1) * block, :], -sin_ref[a * block : (a + 1) * block, :]
        for h in range(heads):
            dq_to[here, h * HEAD : (h + 1) * HEAD] = (
                turn(dq_n[h, there, :], cosine, sine) * scale
            ).astype(BF16)
        dk = turn(dk_n[there, :], cosine, sine)
        dv = dv_n[there, :]
        keep_to[here, :] = jnp.where(first, dk, dv)
        send_to[here, :] = jnp.where(first, dv, dk).astype(BF16)


def attn_backward(starts, q, own, got, d_out, out, lse, lo, hi, cosine, sine, slot):
    half, q_cols = q[0].shape
    heads = q_cols // HEAD
    seq = 2 * half
    pair = lambda cols, dtype: [jax.ShapeDtypeStruct((half, cols), dtype)] * 2
    return pl.pallas_call(
        functools.partial(attn_backward_kernel, slot, seq // 16),
        out_shape=tuple(pair(q_cols, BF16) + pair(HEAD, F32) + pair(HEAD, BF16)),
        in_specs=[ANY_SMEM] + [ANY_VMEM] * 15,
        out_specs=(ANY_VMEM,) * 6,
        scratch_shapes=[
            pltpu.VMEM((heads, seq, HEAD), BF16),
            pltpu.VMEM((1, seq, HEAD), BF16),
            pltpu.VMEM((1, seq, HEAD), BF16),
            pltpu.VMEM((heads, seq, HEAD), BF16),
            pltpu.VMEM((heads, seq, HEAD), BF16),
            pltpu.VMEM((HEAD, seq), BF16),
            pltpu.VMEM((heads, seq, HEAD), F32),
            pltpu.VMEM((seq, HEAD), F32),
            pltpu.VMEM((seq, HEAD), F32),
        ],
        cost_estimate=pl.CostEstimate(
            flops=24 * seq * seq * q_cols, bytes_accessed=seq * q_cols * 16, transcendentals=heads * seq * seq
        ),
        name="attn_backward",
    )(starts, *q, *own, *got, *d_out, *out, lse, lo, hi, cosine, sine)


def hidden_kernel(ff, w_ref, n2_ref, df_ref, *rest):
    out_ref = rest[-1]
    dh = dot(w_ref[2 * ff :, :], df_ref[...], 1, 1)
    gu = dot(w_ref[: 2 * ff, :], n2_ref[...], 1, 1)
    gate, up = gu[:ff], gu[ff:]
    sig = jax.nn.sigmoid(gate)
    silu = gate * sig
    out_ref[:ff, :] = (dh * up * (sig * (1.0 + gate * (1.0 - sig)))).astype(BF16)
    out_ref[ff : 2 * ff, :] = (dh * silu).astype(BF16)
    out_ref[2 * ff :, :] = (silu * up).astype(BF16)


def hidden_half(w, n2, df, *others):
    rows, width = n2.shape
    ff = w.shape[0] // 3
    tile = rows // 3
    return pl.pallas_call(
        functools.partial(hidden_kernel, ff),
        out_shape=jax.ShapeDtypeStruct((3 * ff, rows), BF16),
        grid=(rows // tile,),
        in_specs=[
            pl.BlockSpec((3 * ff, width), lambda r: (0, 0), pipeline_mode=pl.Buffered(1)),
            pl.BlockSpec((tile, width), lambda r: (r, 0)),
            pl.BlockSpec((tile, width), lambda r: (r, 0)),
        ]
        + [pl.BlockSpec(memory_space=pl.ANY)] * len(others),
        out_specs=pl.BlockSpec((3 * ff, tile), lambda r: (0, r)),
        cost_estimate=pl.CostEstimate(
            flops=6 * rows * width * ff, bytes_accessed=6 * ff * width, transcendentals=ff * rows
        ),
        name="hidden",
    )(w, n2, df, *others)


def grads_kernel(ff, lm_ref, lo_ref, nm_ref, no_ref, dm_ref, do_ref, out_ref):
    out_ref[: 2 * ff, :] = (
        dot(lm_ref[: 2 * ff, :], nm_ref[...], 1, 0) + dot(lo_ref[: 2 * ff, :], no_ref[...], 1, 0)
    ).astype(BF16)
    out_ref[2 * ff :, :] = (
        dot(lm_ref[2 * ff :, :], dm_ref[...], 1, 0) + dot(lo_ref[2 * ff :, :], do_ref[...], 1, 0)
    ).astype(BF16)


def feed_grads(left, n2, df):
    rows, half = left[0].shape
    width = n2[0].shape[1]
    tile = 256
    whole = pl.BlockSpec((rows, half), lambda j: (0, 0), pipeline_mode=pl.Buffered(1))
    part = pl.BlockSpec((half, tile), lambda j: (0, j))
    return pl.pallas_call(
        functools.partial(grads_kernel, rows // 3),
        out_shape=jax.ShapeDtypeStruct((rows, width), BF16),
        grid=(width // tile,),
        in_specs=[whole, whole, part, part, part, part],
        out_specs=pl.BlockSpec((rows, tile), lambda j: (0, j)),
        cost_estimate=pl.CostEstimate(
            flops=4 * rows * half * width, bytes_accessed=rows * width * 2, transcendentals=0
        ),
        name="feed_grads",
    )(*left, *n2, *df)


def add_last_kernel(a0, b0, a1, b1, *rest):
    out, rows = rest[-1], b0.shape[0]
    out[:rows, :] = a0[:rows, :].astype(F32) + b0[...].astype(F32)
    out[rows:, :] = a1[:rows, :].astype(F32) + b1[...].astype(F32)


def collect_end_after(state, *others):
    one, two = state
    h, width = one.shape[0] // 2, one.shape[1]
    return pl.pallas_call(
        add_last_kernel,
        out_shape=jax.ShapeDtypeStruct((2 * h, width), F32),
        in_specs=[ANY_VMEM] * 4 + [pl.BlockSpec(memory_space=pl.ANY)] * len(others),
        out_specs=ANY_VMEM,
        name="add_last",
    )(one, side(one[h:]), two, far(two[h:]), *others)


def hold_kernel(v_ref, *rest):
    rest[-1][...] = v_ref[...]


def hold(v, *others):
    rows, width = v.shape
    tile = rows // 3 if rows % 48 == 0 else rows
    return pl.pallas_call(
        hold_kernel,
        out_shape=jax.ShapeDtypeStruct(v.shape, v.dtype),
        grid=(rows // tile,),
        in_specs=[pl.BlockSpec((tile, width), lambda i: (i, 0))] + [pl.BlockSpec(memory_space=pl.ANY)] * len(others),
        out_specs=pl.BlockSpec((tile, width), lambda i: (i, 0)),
        name="hold",
    )(v, *others)


def bring(c_ref, first, rows, refs, buf, sems):
    copies = [
        pltpu.make_async_copy(
            ref.at[pl.ds(start, rows), :], buf.at[lax.bitwise_xor(c_ref[0], bits)], sems.at[bits]
        )
        for bits, (ref, start) in enumerate(zip(refs, first))
    ]
    for copy in copies:
        copy.start()
    for copy in copies:
        copy.wait()


def finish_kernel(turned, sizes, c_ref, *refs):
    parts = len(sizes)
    pieces, out_ref, bufs, sems = refs[: 4 * parts], refs[4 * parts], refs[4 * parts + 1 : -1], refs[-1]
    for part, rows in enumerate(sizes):
        bring(c_ref, turned[1][part], rows, pieces[4 * part : 4 * part + 4], bufs[part], sems.at[part])
    at = 0
    for k in range(4):
        for part, rows in enumerate(sizes):
            v = bufs[part][k].astype(F32)
            if turned[0]:
                out_ref[:, at : at + rows] = v.T
            else:
                out_ref[at : at + rows, :] = v
            at += rows


def finish(c, sizes, turned, parts):
    width = parts[0][0][0].shape[1]
    total = 4 * sum(sizes)
    shape = (width, total) if turned else (total, width)
    firsts = [[first for _, first in part] for part in parts]
    return pl.pallas_call(
        functools.partial(finish_kernel, (turned, firsts), sizes),
        out_shape=jax.ShapeDtypeStruct(shape, F32),
        in_specs=[ANY_SMEM] + [pl.BlockSpec(memory_space=pl.ANY)] * (4 * len(parts)),
        out_specs=ANY_VMEM,
        scratch_shapes=[pltpu.VMEM((4, rows, width), BF16) for rows in sizes]
        + [pltpu.SemaphoreType.DMA((len(parts), 4))],
        name="finish",
    )(c, *[v for part in parts for v, _ in part])


def finish_attn_kernel(q_cols, c_ref, r0, r1, r2, r3, q_ref, k_ref, v_ref, o_ref, gain_ref, buf, sems):
    rows = buf.shape[1]
    bring(c_ref, (0,) * 4, rows, (r0, r1, r2, r3), buf, sems)
    qkv = q_cols + HEAD
    for k in range(4):
        q_ref[:, k * q_cols : (k + 1) * q_cols] = buf[k, :q_cols, :].astype(F32).T
        to = v_ref if k % 2 else k_ref
        to[:, (k // 2) * HEAD : (k // 2 + 1) * HEAD] = buf[k, q_cols:qkv, :].astype(F32).T
        o_ref[k * q_cols : (k + 1) * q_cols, :] = buf[k, qkv + 16 :, :].astype(F32)
    gain_ref[...] = sum(buf[k, qkv : qkv + 16, :].astype(F32) for k in range(4))


def finish_attn(c, q_cols, pieces):
    rows, width = pieces[0].shape
    shapes = [(width, 4 * q_cols), (width, 2 * HEAD), (width, 2 * HEAD), (4 * q_cols, width), (16, width)]
    return pl.pallas_call(
        functools.partial(finish_attn_kernel, q_cols),
        out_shape=tuple(jax.ShapeDtypeStruct(shape, F32) for shape in shapes),
        in_specs=[ANY_SMEM] + [pl.BlockSpec(memory_space=pl.ANY)] * 4,
        out_specs=(ANY_VMEM,) * 5,
        scratch_shapes=[pltpu.VMEM((4, rows, width), BF16), pltpu.SemaphoreType.DMA((4,))],
        name="finish_attn",
    )(c, *pieces)


def tables(c, t, core, tok_rows, seq_ids, pic_starts, pic_lengths):
    seq_len = seq_ids.shape[1]
    start_list = arrival_starts(c, t, tok_rows)
    starts = jnp.stack(start_list + [core]).astype(jnp.int32)
    positions = (starts[:16, None] + jnp.arange(seq_len // 16, dtype=jnp.int32)[None, :]).reshape(-1)
    frequency = jnp.power(rope_base, -jnp.arange(HEAD // 2, dtype=F32) * 2.0 / HEAD)
    angles = positions.astype(F32)[:, None] * frequency[None, :]
    cosine, sine = jnp.cos(angles), jnp.sin(angles)
    cosine = jnp.concatenate([cosine, cosine], axis=1)
    sine = jnp.concatenate([-sine, sine], axis=1)
    docs = seq_ids[0]
    index = jnp.arange(seq_len, dtype=jnp.int32)
    lo = jnp.sum((docs[:, None] < docs[None, :]).astype(jnp.int32), axis=0)
    doc_end = jnp.sum((docs[:, None] <= docs[None, :]).astype(jnp.int32), axis=0) - 1
    pic_ends = pic_starts[0] + pic_lengths[0]
    inside = (index[:, None] >= pic_starts[0][None, :]) & (index[:, None] < pic_ends[None, :])
    last = jnp.max(jnp.where(inside, pic_ends[None, :] - 1, -1), axis=1)
    hi = jnp.minimum(doc_end, jnp.maximum(index, last))
    lo, hi = lo[None, :], hi[None, :]
    return starts, cosine, sine, lo, hi


def body(
    tokens,
    seq_ids,
    pic_starts,
    pic_lengths,
    skip_mask,
    w_query,
    w_key,
    w_value,
    w_out,
    w_gate,
    w_up,
    w_down,
    gain_attn,
    gain_ffn,
    cotangent,
):
    tok_rows = tokens.shape[1]
    own = tok_rows // 2
    seq_len = seq_ids.shape[1]
    slot = seq_len // pic_starts.shape[1]
    c = lax.axis_index("ctx")
    t = lax.axis_index("tp")
    core = (c & 1).astype(jnp.int32)
    q_cols = w_query.shape[1] // 4
    ff = w_gate.shape[1] // 4
    part_a = (ff * 3 // 4 + 15) // 16 * 16
    part_b = ff - part_a

    flag = seq_ids[0, 0] >= 0
    qkv_cols = q_cols + HEAD
    half = seq_len // 2
    core_flag = core.reshape(1)
    first_own = pack_first(
        jnp.stack([c, core, c >> 1]).astype(jnp.int32), w_query, w_key, w_value, w_out, gain_attn, gain_ffn
    )
    first = gather_whole(first_own)

    def start_stage(tokens, skip_mask, cotangent, w_gate, w_up, w_down, seq_ids, pic_starts, pic_lengths):
        x_own_b = lax.dynamic_slice_in_dim(tokens[0], t * own, own, 0)
        keep_own = lax.dynamic_slice_in_dim(skip_mask[0], t * own, own, 0).astype(F32)[:, None]
        dy_own = lax.dynamic_slice_in_dim(cotangent[0], t * own, own, 0).astype(F32)
        parts = spread_start(x_own_b)
        wd_own = lax.dynamic_slice_in_dim(w_down, c * ff, ff, 0)
        wg_t = lax.dynamic_slice_in_dim(w_gate, c * ff, ff, 1).T
        wu_t = lax.dynamic_slice_in_dim(w_up, c * ff, ff, 1).T
        weights = [
            jnp.concatenate([v[first:last] for v in (wg_t, wu_t, wd_own)], axis=0)
            for first, last in ((0, part_a), (part_a, ff))
        ]
        parts = after(parts, weights)
        ready = parts[:2] + spread_more(parts)
        table = tables(c, t, core, tok_rows, seq_ids, pic_starts, pic_lengths)
        d_ffn_own = (keep_own * dy_own).astype(BF16)
        x_mine = spread_join(after(ready, table, d_ffn_own))
        x_other = near(x_mine)
        return x_own_b.astype(F32), keep_own, dy_own, d_ffn_own, x_mine, x_other, weights, table

    x_own, keep_own, dy_own, d_ffn_own, x_mine, x_other, weights, (starts, cosine, sine, lo, hi) = fenced(
        flag, start_stage,
        *after((tokens, skip_mask, cotangent, w_gate, w_up, w_down, seq_ids, pic_starts, pic_lengths), first_own)
    )
    weights = after(weights, x_other)
    wa, wb = gather_whole(weights[0]), gather_whole(weights[1])

    def forward_stage(x_mine, x_other, first, d_ffn_own, x_own, keep_own, cosine, sine, lo, hi, starts):
        wo = first[qkv_cols + 16 :]
        gain_two = first[qkv_cols + 1 : qkv_cols + 2].astype(F32)
        df_parts = spread_start(d_ffn_own)
        n1m, qm, kvm = qkv_half(core_flag, x_mine, first, qkv_cols, cosine[:half], sine[:half])
        n1o, qo, kvo = qkv_half(core_flag, x_other, first, qkv_cols, cosine[half:], sine[half:])
        q, own_kv = (qm, qo), (kvm, kvo)
        got = (near(kvo), near(kvm))
        q = after(q, df_parts)
        df_ready = df_parts[:2] + spread_more(df_parts)
        hm, ho, lse = attn_forward(starts, q, own_kv, got, lo, hi, slot)
        hm, ho = after((hm, ho), df_ready)
        both = join_cores(dot(hm, wo, 1, 0).astype(BF16), dot(ho, wo, 1, 0).astype(BF16))
        state = collect_first(both)
        dfm = spread_join(after(df_ready, both))
        attn = collect_end(collect_second(after(state, dfm)))
        dfo = near(dfm)
        mid = x_own + keep_own * attn
        inv_two = lax.rsqrt(jnp.mean(mid * mid, axis=-1, keepdims=True) + norm_eps)
        hat_two = mid * inv_two
        n2m, n2o = spread((hat_two * gain_two).astype(BF16))
        return n1m, n1o, q, own_kv, got, hm, ho, lse, dfm, dfo, n2m, n2o, mid, inv_two, hat_two

    n1m, n1o, q, own_kv, got, hm, ho, lse, dfm, dfo, n2m, n2o, mid, inv_two, hat_two = fenced(
        flag, forward_stage, x_mine, x_other, first, d_ffn_own, x_own, keep_own, cosine, sine, lo, hi, starts
    )

    am, ao = hidden_half(wa, n2m, dfm), hidden_half(wa, n2o, dfo)
    grad_a = feed_grads((am, ao), (n2m, n2o), (dfm, dfo))
    shard_a = scatter_whole(grad_a)
    pao = dot(ao[: 2 * part_a], wa[: 2 * part_a], 0, 0).astype(BF16)
    bm, bo = hidden_half(wb, n2m, dfm, pao), hidden_half(wb, n2o, dfo, pao)
    grad_b = feed_grads((bm, bo), (n2m, n2o), (dfm, dfo))
    shard_b = scatter_whole(grad_b)

    def middle_stage(am, ao, bm, bo, pao, wa, wb, first, dy_own, keep_own, hat_two, inv_two):
        gain_two = first[qkv_cols + 1 : qkv_cols + 2].astype(F32)
        p_other = (pao.astype(F32) + dot(bo[: 2 * part_b], wb[: 2 * part_b], 0, 0)).astype(BF16)
        p_mine = (
            dot(am[: 2 * part_a], wa[: 2 * part_a], 0, 0) + dot(bm[: 2 * part_b], wb[: 2 * part_b], 0, 0)
        ).astype(BF16)
        both = join_cores(p_mine, p_other)
        state = collect_first(both)
        am, ao, bm, bo = after((am, ao, bm, bo), both)

        def feed_out(a, b):
            return (
                dot(a[2 * part_a :], wa[2 * part_a :], 0, 0) + dot(b[2 * part_b :], wb[2 * part_b :], 0, 0)
            ).astype(BF16)

        f_other, f_mine = feed_out(ao, bo), feed_out(am, bm)
        d_n2 = collect_end(collect_second(after(state, f_other, f_mine)))
        d_mid = dy_own + norm_back(d_n2, hat_two, inv_two, gain_two)
        share_two = jnp.sum(d_n2 * hat_two, axis=0, keepdims=True)
        f_split = collect_split(join_cores(f_mine, f_other))
        dam, dao = spread((keep_own * d_mid).astype(BF16), f_split)
        d_head_m = dot(dam, first[qkv_cols + 16 :], 1, 1).astype(BF16)
        return d_mid, share_two, dam, dao, f_split, d_head_m

    bm, bo = after((bm, bo), grad_b)
    d_mid, share_two, dam, dao, f_split, d_head_m = fenced(
        flag, middle_stage, am, ao, bm, bo, pao, wa, wb, first, dy_own, keep_own, hat_two, inv_two
    )

    def backward_stage(
        share_two, dam, dao, f_split, d_head_m, first, q, own_kv, got, hm, ho, lse, lo, hi, cosine, sine, starts,
        x_mine, x_other, n1m, n1o, shard_a
    ):
        wqkv, wo = first[:qkv_cols], first[qkv_cols + 16 :]
        f_state = collect_send(f_split)
        d_head = (d_head_m, dot(dao, wo, 1, 1).astype(BF16))
        dqm, dqo, keepm, keepo, sendm, sendo = attn_backward(
            starts, q, own_kv, got, d_head, (hm, ho), lse, lo, hi, cosine, sine, slot
        )
        sendm, sendo = after((sendm, sendo), f_state)
        a_far = far(shard_a[: 2 * part_a])
        got_m, got_o = near(sendo), near(sendm)
        do = jnp.concatenate([dqo, (keepo + got_o.astype(F32)).astype(BF16)], axis=1)
        e_other = dot(do, wqkv, 1, 0).astype(BF16)
        dm = jnp.concatenate([dqm, (keepm + got_m.astype(F32)).astype(BF16)], axis=1)
        e_mine = dot(dm, wqkv, 1, 0).astype(BF16)
        both = join_cores(e_mine, e_other)
        state = collect_first(both)
        dm, do, hm, ho, x_mine, x_other = after((dm, do, hm, ho, x_mine, x_other), both)
        grad_qkv = (dot(dm, n1m, 0, 0) + dot(do, n1o, 0, 0)).astype(BF16)

        def gain_share(e, x):
            x = x.astype(F32)
            inv = lax.rsqrt(jnp.mean(x * x, axis=-1, keepdims=True) + norm_eps)
            return jnp.sum(e.astype(F32) * (x * inv), axis=0, keepdims=True)

        share_one = gain_share(e_mine, x_mine) + gain_share(e_other, x_other)
        shares = jnp.concatenate(
            [share_one, share_two, jnp.zeros((14, share_one.shape[1]), F32)], axis=0
        )
        shares_side = side(shares.astype(BF16))
        state = collect_second(after(state, grad_qkv, shares))
        hm, ho, dam, dao = after((hm, ho, dam, dao), state)
        grad_out = (dot(hm, dam, 0, 0) + dot(ho, dao, 0, 0)).astype(BF16)
        shares = (shares + shares_side.astype(F32)).astype(BF16)
        grad_attn = jnp.concatenate([grad_qkv, shares, grad_out], axis=0)
        d_n1 = collect_end_after(state, grad_out)
        return d_n1, grad_attn, collect_second(f_state), a_far

    d_n1, grad_attn, f_state, a_far = fenced(
        flag, backward_stage, share_two, dam, dao, f_split, d_head_m, first, q, own_kv, got, hm, ho, lse, lo, hi,
        cosine, sine, starts, x_mine, x_other, n1m, n1o, shard_a
    )
    shard_attn = scatter_whole(after(grad_attn, shard_b))
    member = c.astype(jnp.int32).reshape(1)

    def end_stage(d_n1, f_state, x_own, d_mid, first, mid, keep_own, shard_a, a_far, shard_b):
        gain_one = first[qkv_cols : qkv_cols + 1].astype(F32)
        ffn = collect_end(f_state)
        inv_one = lax.rsqrt(jnp.mean(x_own * x_own, axis=-1, keepdims=True) + norm_eps)
        hat_one = x_own * inv_one
        input_grad = (d_mid + norm_back(d_n1, hat_one, inv_one, gain_one)).astype(BF16)
        output = (mid + keep_own * ffn).astype(BF16)
        gate_far = far(hold(shard_b[:part_b], ffn))
        a_near, a_near_far, b_near = near(shard_a), near(a_far), near(shard_b)
        grad_gate = finish(
            member, sizes, True,
            [
                [(shard_a, 0), (a_near, 0), (a_far, 0), (a_near_far, 0)],
                [(shard_b, 0), (b_near, 0), (gate_far, 0), (near(gate_far), 0)],
            ],
        )
        rest = jnp.concatenate([shard_a[2 * part_a :], shard_b[part_b:]], axis=0)
        rest_far = hold(far(hold(rest, ffn)), grad_gate)
        return (
            in_order(input_grad, side(input_grad), t), output, grad_gate, a_near, a_near_far, b_near, rest_far, near(rest_far)
        )

    sizes = (part_a, part_b)
    input_grad, output, grad_gate, a_near, a_near_far, b_near, rest_far, near_far = fenced(
        flag, end_stage, d_n1, f_state, x_own, d_mid, first, mid, keep_own, shard_a, a_far, shard_b
    )

    def last_stage(shard_a, shard_b, a_near, a_far, a_near_far, b_near, rest_far, near_far, shard_attn, output):
        attn_far = far(shard_attn)
        up = [
            [(shard_a, part_a), (a_near, part_a), (a_far, part_a), (a_near_far, part_a)],
            [(shard_b, part_b), (b_near, part_b), (rest_far, part_a), (near_far, part_a)],
        ]
        down = [
            [(shard_a, 2 * part_a), (a_near, 2 * part_a), (rest_far, 0), (near_far, 0)],
            [(shard_b, 2 * part_b), (b_near, 2 * part_b), (rest_far, part_a + part_b), (near_far, part_a + part_b)],
        ]
        feed = finish(member, sizes, True, up), finish(member, sizes, False, down)
        attn_far = hold(attn_far, *feed)
        return feed, in_order(output, side(output), t), finish_attn(
            member, q_cols, (shard_attn, near(shard_attn), attn_far, near(attn_far))
        )

    (grad_up, grad_down), output, (grad_query, grad_key, grad_value, grad_out, gain_grads) = fenced(
        flag, last_stage, shard_a, shard_b, a_near, a_far, a_near_far, b_near, rest_far, near_far, shard_attn, output
    )
    return (
        output[None],
        input_grad[None],
        grad_query,
        grad_key,
        grad_value,
        grad_out,
        grad_gate,
        grad_up,
        grad_down,
        gain_grads[0],
        gain_grads[1],
    )


def solution(mesh):
    placed = (
        P("fsdp", "ctx", None),
        P("fsdp", None),
        P("fsdp", None),
        P("fsdp", None),
        P("fsdp", "ctx"),
        P("fsdp", "tp"),
        P("fsdp", "tp"),
        P("fsdp", "tp"),
        P("tp", "fsdp"),
        P("fsdp", "tp"),
        P("fsdp", "tp"),
        P("tp", "fsdp"),
        P("fsdp"),
        P("fsdp"),
        P("fsdp", "ctx", None),
    )
    return jax.shard_map(
        body,
        mesh=mesh,
        in_specs=placed,
        out_specs=(
            P("fsdp", "ctx", None),
            P("fsdp", "ctx", None),
            P("fsdp", "tp"),
            P("fsdp", "tp"),
            P("fsdp", "tp"),
            P("tp", "fsdp"),
            P("fsdp", "tp"),
            P("fsdp", "tp"),
            P("tp", "fsdp"),
            P("fsdp"),
            P("fsdp"),
        ),
        check_vma=False,
    )
```

```python
import functools
import math

import jax
import jax.numpy as jnp
from jax import lax
from jax.experimental import pallas as pl
from jax.experimental.pallas import tpu as pltpu
from jax.sharding import PartitionSpec as P

HEAD = 128
norm_eps = 1e-05
rope_base = 10000.0
F32 = jnp.float32
BF16 = jnp.bfloat16
ANY_VMEM = pl.BlockSpec(memory_space=pltpu.VMEM)
ANY_SMEM = pl.BlockSpec(memory_space=pltpu.SMEM)


def dot(a, b, ca, cb):
    return lax.dot_general(a, b, (((ca,), (cb,)), ((), ())), preferred_element_type=F32)


def after(v, *others):
    return lax.optimization_barrier((v,) + others)[0] if others else v


def fenced(flag, stage, *values):
    shapes = jax.eval_shape(stage, *values)

    def empty(*_):
        return jax.tree.map(lambda a: jnp.zeros(a.shape, a.dtype), shapes)

    return lax.cond(flag, stage, empty, *values)


def norm_back(d_normed, hat, inv_rms, gain):
    scaled = d_normed * gain
    return inv_rms * (scaled - hat * jnp.mean(scaled * hat, axis=-1, keepdims=True))


def far(v):
    return lax.ppermute(v, "ctx", [(i, i ^ 2) for i in range(4)])


def near(v):
    return lax.ppermute(v, "ctx", [(i, i ^ 1) for i in range(4)])


def side(v):
    return lax.ppermute(v, "tp", [(0, 1), (1, 0)])


def join_kernel(count, *refs):
    pieces, out_ref, sem = refs[:count], refs[-2], refs[-1]
    copies, row = [], 0
    for k, piece in enumerate(pieces):
        n = piece.shape[0]
        copies.append(pltpu.make_async_copy(piece, out_ref.at[pl.ds(row, n), :], sem.at[k]))
        copies[-1].start()
        row += n
    for copy in copies:
        copy.wait()


def join(*pieces, others=()):
    rows = sum(p.shape[0] for p in pieces)
    return pl.pallas_call(
        functools.partial(join_kernel, len(pieces)),
        out_shape=jax.ShapeDtypeStruct((rows, pieces[0].shape[1]), pieces[0].dtype),
        in_specs=[pl.BlockSpec(memory_space=pl.ANY)] * (len(pieces) + len(others)),
        out_specs=ANY_VMEM,
        scratch_shapes=[pltpu.SemaphoreType.DMA((len(pieces),))],
        name="join",
    )(*pieces, *others)


def spread_start(v):
    h = v.shape[0] // 2
    one, two = v[:h], v[h:]
    return one, two, far(one), side(two), side(one), far(two)


def spread_more(parts):
    one, two, one_far, two_side, one_side, two_far = parts
    return one_far, two_side, one_side, two_far, side(one_far), far(two_side)


def spread_join(ready, others=()):
    one, two, one_far, two_side, one_side, two_far, one_both, two_both = ready
    return join(one, one_far, one_side, one_both, two, two_side, two_far, two_both, others=others)


def spread(v, others=()):
    parts = spread_start(v)
    mine = spread_join(parts[:2] + spread_more(parts), others)
    return mine, near(mine)


def arrival_starts(c, t, tok_rows):
    own = tok_rows // 2
    starts = []
    for near_bit in range(2):
        for second in range(2):
            order = ((0, 0), (1, 0), (0, 1), (1, 1)) if second == 0 else ((0, 0), (0, 1), (1, 0), (1, 1))
            for far_bit, side_bit in order:
                ctx = c ^ (near_bit + 2 * far_bit)
                starts.append(ctx * tok_rows + (t ^ side_bit) * own + second * (own // 2))
    return starts


def collect_split(both):
    h = both.shape[0] // 8
    one = both[: 4 * h].reshape(2, 2, h, -1)
    two = both[4 * h :].reshape(2, 2, h, -1)
    return [v[:, k].reshape(2 * h, -1) for k in range(2) for v in (one, two)]


def collect_send(split):
    one, two, one_sent, two_sent = split
    return one, two, far(one_sent), side(two_sent)


def collect_first(both):
    return collect_send(collect_split(both))


def collect_second(state):
    one, two, one_far, two_side = state
    return add(one, one_far), add(two, two_side)


def collect_start(p_mine, p_other):
    return collect_second(collect_first(join_cores(p_mine, p_other)))


def join_cores(p_mine, p_other):
    return add(lax.optimization_barrier(p_mine), near(p_other))


def collect_end(state):
    one, two = state
    h = one.shape[0] // 2
    one_side = side(one[h:])
    two_far = far(two[h:])
    return jnp.concatenate(
        [
            one[:h].astype(F32) + one_side.astype(F32),
            two[:h].astype(F32) + two_far.astype(F32),
        ],
        axis=0,
    )


def collect(p_mine, p_other):
    return collect_end(collect_start(p_mine, p_other))


def in_order(v, other, t):
    return jnp.where(
        t == 0, jnp.concatenate([v, other], axis=0), jnp.concatenate([other, v], axis=0)
    )


def gather_whole(v):
    return lax.all_gather(v, "fsdp", axis=1, tiled=True)


def scatter_whole(g):
    return lax.psum_scatter(g, "fsdp", scatter_dimension=1, tiled=True)


def add(a, b):
    return (a.astype(F32) + b.astype(F32)).astype(BF16)


def pack_first_kernel(at_ref, wq_ref, wk_ref, wv_ref, wo_ref, one_ref, two_ref, out_ref):
    q_cols = wq_ref.shape[1]
    qkv = q_cols + HEAD
    out_ref[:q_cols, :] = wq_ref[...].astype(F32).T.astype(BF16)
    w_kv = jnp.where(at_ref[1] == 0, wk_ref[...].astype(F32), wv_ref[...].astype(F32))
    out_ref[q_cols:qkv, :] = w_kv.T.astype(BF16)
    row = lax.broadcasted_iota(jnp.int32, (16, out_ref.shape[1]), 0)
    one, two = one_ref[...].astype(F32)[None, :], two_ref[...].astype(F32)[None, :]
    out_ref[qkv : qkv + 16, :] = jnp.where(row == 0, one, jnp.where(row == 1, two, 0.0)).astype(BF16)
    out_ref[qkv + 16 :, :] = wo_ref[...]


def pack_first(at, w_query, w_key, w_value, w_out, gain_one, gain_two):
    depth = w_query.shape[0]
    q_cols = w_query.shape[1] // 4
    rows = 2 * q_cols + HEAD + 16
    gain = pl.BlockSpec((depth,), lambda i, at: (0,))
    return pl.pallas_call(
        pack_first_kernel,
        out_shape=jax.ShapeDtypeStruct((rows, depth), BF16),
        grid_spec=pltpu.PrefetchScalarGridSpec(
            num_scalar_prefetch=1,
            grid=(1,),
            in_specs=[
                pl.BlockSpec((depth, q_cols), lambda i, at: (0, at[0])),
                pl.BlockSpec((depth, HEAD), lambda i, at: (0, at[2])),
                pl.BlockSpec((depth, HEAD), lambda i, at: (0, at[2])),
                pl.BlockSpec((q_cols, depth), lambda i, at: (at[0], 0)),
                gain,
                gain,
            ],
            out_specs=pl.BlockSpec((rows, depth), lambda i, at: (0, 0)),
        ),
        name="pack_first",
    )(at, w_query, w_key, w_value, w_out, gain_one, gain_two)


def turn(u, cosine, sine):
    return u * cosine + pltpu.roll(u, HEAD // 2, 1) * sine


def qkv_kernel(heads, core_ref, x_ref, w_ref, gain_ref, cos_ref, sin_ref, n1_ref, q_ref, kv_ref):
    x = x_ref[...].astype(F32)
    inv = lax.rsqrt(jnp.mean(x * x, axis=-1, keepdims=True) + norm_eps)
    n1 = (x * inv * gain_ref[0:1, :].astype(F32)).astype(BF16)
    n1_ref[...] = n1
    pre = dot(n1, w_ref[...], 1, 1)
    cosine, sine = cos_ref[...], sin_ref[...]
    scale = 1.0 / math.sqrt(HEAD)
    for h in range(heads):
        u = pre[:, h * HEAD : (h + 1) * HEAD]
        q_ref[:, h * HEAD : (h + 1) * HEAD] = (turn(u, cosine, sine) * scale).astype(BF16)
    u = pre[:, heads * HEAD :]
    kv_ref[...] = jnp.where(core_ref[0] == 0, turn(u, cosine, sine), u).astype(BF16)


def qkv_half(core, x, first, cols, cosine, sine):
    rows, width = x.shape
    heads = cols // HEAD - 1
    tile = rows // 3
    return pl.pallas_call(
        functools.partial(qkv_kernel, heads),
        out_shape=(
            jax.ShapeDtypeStruct((rows, width), BF16),
            jax.ShapeDtypeStruct((rows, heads * HEAD), BF16),
            jax.ShapeDtypeStruct((rows, HEAD), BF16),
        ),
        grid=(rows // tile,),
        in_specs=[
            ANY_SMEM,
            pl.BlockSpec((tile, width), lambda r: (r, 0)),
            pl.BlockSpec((cols, width), lambda r: (0, 0)),
            pl.BlockSpec((16, width), lambda r: (cols // 16, 0)),
            pl.BlockSpec((tile, HEAD), lambda r: (r, 0)),
            pl.BlockSpec((tile, HEAD), lambda r: (r, 0)),
        ],
        out_specs=(
            pl.BlockSpec((tile, width), lambda r: (r, 0)),
            pl.BlockSpec((tile, heads * HEAD), lambda r: (r, 0)),
            pl.BlockSpec((tile, HEAD), lambda r: (r, 0)),
        ),
        cost_estimate=pl.CostEstimate(
            flops=2 * rows * width * cols, bytes_accessed=rows * width * 4 + cols * width * 2, transcendentals=0
        ),
        name="qkv",
    )(core, x, first, first, cosine, sine)


def to_order(starts_ref, mine, other, dest, block):
    per = mine.shape[0] // block
    for a in range(2 * per):
        src = mine if a < per else other
        at = pl.multiple_of(starts_ref[a], block)
        row = (a % per) * block
        for h in range(dest.shape[0]):
            dest[h, pl.ds(at, block), :] = src[row : row + block, h * HEAD : (h + 1) * HEAD]


def keys_in_order(starts_ref, own, got, k_n, v_n, block):
    @pl.when(starts_ref[16] == 0)
    def _():
        to_order(starts_ref, *own, k_n, block)
        to_order(starts_ref, *got, v_n, block)

    @pl.when(starts_ref[16] != 0)
    def _():
        to_order(starts_ref, *own, v_n, block)
        to_order(starts_ref, *got, k_n, block)


def over_queries(heads, seq, slot, step, visit, unrolled):
    def one(h, carry):
        for row in range(0, seq, step):
            visit(h, row, (row // slot + 1) * slot)
        return carry

    if unrolled:
        for h in range(heads):
            one(h, 0)
    else:
        lax.fori_loop(0, heads, one, 0)


def attn_forward_kernel(
    slot, block, starts_ref, qm, qo, km, ko, rm, ro, lo_ref, hi_ref, om, oo, lse_ref, q_n, k_n, v_n, o_n, vt_n
):
    heads, seq, _ = q_n.shape
    to_order(starts_ref, qm, qo, q_n, block)
    keys_in_order(starts_ref, (km, ko), (rm, ro), k_n, v_n, block)
    vt_n[...] = v_n[0].astype(F32).T.astype(BF16)
    step = 256

    def visit(h, row, nk):
        rows = pl.ds(row, step)
        s = dot(k_n[0, :nk, :], q_n[h, rows, :], 1, 1)
        j = lax.broadcasted_iota(jnp.int32, s.shape, 0)
        ok = (j >= lo_ref[:, rows]) & (j <= hi_ref[:, rows])
        s = jnp.where(ok, s, -1e30)
        top = jnp.max(s, axis=0, keepdims=True)
        e = jnp.exp(s - top)
        total = jnp.sum(e, axis=0, keepdims=True)
        soft = (e * (1.0 / total)).astype(BF16)
        out = dot(vt_n[:, :nk], soft, 1, 0)
        o_n[h, rows, :] = out.T.astype(BF16)
        lse_ref[h, :, rows] = top + jnp.log(total)

    over_queries(heads, seq, slot, step, visit, False)
    per = om.shape[0] // block
    for a in range(2 * per):
        dest = om if a < per else oo
        row = (a % per) * block
        for h in range(heads):
            dest[row : row + block, h * HEAD : (h + 1) * HEAD] = o_n[
                h, pl.ds(pl.multiple_of(starts_ref[a], block), block), :
            ]


def attn_forward(starts, q, own, got, lo, hi, slot):
    half, q_cols = q[0].shape
    heads = q_cols // HEAD
    seq = 2 * half
    return pl.pallas_call(
        functools.partial(attn_forward_kernel, slot, seq // 16),
        out_shape=(
            jax.ShapeDtypeStruct((half, q_cols), BF16),
            jax.ShapeDtypeStruct((half, q_cols), BF16),
            jax.ShapeDtypeStruct((heads, 1, seq), F32),
        ),
        in_specs=[ANY_SMEM] + [ANY_VMEM] * 8,
        out_specs=(ANY_VMEM, ANY_VMEM, ANY_VMEM),
        scratch_shapes=[
            pltpu.VMEM((heads, seq, HEAD), BF16),
            pltpu.VMEM((1, seq, HEAD), BF16),
            pltpu.VMEM((1, seq, HEAD), BF16),
            pltpu.VMEM((heads, seq, HEAD), BF16),
            pltpu.VMEM((HEAD, seq), BF16),
        ],
        cost_estimate=pl.CostEstimate(
            flops=12 * seq * seq * q_cols, bytes_accessed=seq * q_cols * 8, transcendentals=heads * seq * seq
        ),
        name="attn_forward",
    )(starts, q[0], q[1], own[0], own[1], got[0], got[1], lo, hi)


def attn_backward_kernel(
    slot, block, starts_ref, qm, qo, km, ko, rm, ro, dom, doo, om, oo, lse_ref, lo_ref, hi_ref, cos_ref, sin_ref,
    dqm, dqo, keepm, keepo, sendm, sendo, q_n, k_n, v_n, do_n, o_n, kt_n, dq_n, dk_n, dv_n,
):
    heads, seq, _ = q_n.shape
    to_order(starts_ref, qm, qo, q_n, block)
    to_order(starts_ref, dom, doo, do_n, block)
    to_order(starts_ref, om, oo, o_n, block)
    keys_in_order(starts_ref, (km, ko), (rm, ro), k_n, v_n, block)
    kt_n[...] = k_n[0].astype(F32).T.astype(BF16)
    dk_n[...] = jnp.zeros_like(dk_n)
    dv_n[...] = jnp.zeros_like(dv_n)
    step = slot

    def visit(h, row, nk):
        rows = pl.ds(row, step)
        q = q_n[h, rows, :]
        d_out = do_n[h, rows, :]
        s = dot(k_n[0, :nk, :], q, 1, 1)
        j = lax.broadcasted_iota(jnp.int32, s.shape, 0)
        ok = (j >= lo_ref[:, rows]) & (j <= hi_ref[:, rows])
        soft = jnp.exp(jnp.where(ok, s - lse_ref[h, :, rows], -1e30))
        d_soft = dot(v_n[0, :nk, :], d_out, 1, 1)
        delta = jnp.sum((d_out.astype(F32) * o_n[h, rows, :].astype(F32)).T, axis=0, keepdims=True)
        d_s = (soft * (d_soft - delta)).astype(BF16)
        dv_n[:nk, :] += dot(soft.astype(BF16), d_out, 1, 0)
        dk_n[:nk, :] += dot(d_s, q, 1, 0)
        dq_n[h, rows, :] = dot(kt_n[:, :nk], d_s, 1, 0).T

    over_queries(heads, seq, slot, step, visit, True)
    per = dqm.shape[0] // block
    scale = 1.0 / math.sqrt(HEAD)
    first = starts_ref[16] == 0
    for a in range(2 * per):
        dq_to, keep_to, send_to = (dqm, keepm, sendm) if a < per else (dqo, keepo, sendo)
        row = (a % per) * block
        here = slice(row, row + block)
        there = pl.ds(pl.multiple_of(starts_ref[a], block), block)
        cosine, sine = cos_ref[a * block : (a + 1) * block, :], -sin_ref[a * block : (a + 1) * block, :]
        for h in range(heads):
            dq_to[here, h * HEAD : (h + 1) * HEAD] = (
                turn(dq_n[h, there, :], cosine, sine) * scale
            ).astype(BF16)
        dk = turn(dk_n[there, :], cosine, sine)
        dv = dv_n[there, :]
        keep_to[here, :] = jnp.where(first, dk, dv)
        send_to[here, :] = jnp.where(first, dv, dk).astype(BF16)


def attn_backward(starts, q, own, got, d_out, out, lse, lo, hi, cosine, sine, slot):
    half, q_cols = q[0].shape
    heads = q_cols // HEAD
    seq = 2 * half
    pair = lambda cols, dtype: [jax.ShapeDtypeStruct((half, cols), dtype)] * 2
    return pl.pallas_call(
        functools.partial(attn_backward_kernel, slot, seq // 16),
        out_shape=tuple(pair(q_cols, BF16) + pair(HEAD, F32) + pair(HEAD, BF16)),
        in_specs=[ANY_SMEM] + [ANY_VMEM] * 15,
        out_specs=(ANY_VMEM,) * 6,
        scratch_shapes=[
            pltpu.VMEM((heads, seq, HEAD), BF16),
            pltpu.VMEM((1, seq, HEAD), BF16),
            pltpu.VMEM((1, seq, HEAD), BF16),
            pltpu.VMEM((heads, seq, HEAD), BF16),
            pltpu.VMEM((heads, seq, HEAD), BF16),
            pltpu.VMEM((HEAD, seq), BF16),
            pltpu.VMEM((heads, seq, HEAD), F32),
            pltpu.VMEM((seq, HEAD), F32),
            pltpu.VMEM((seq, HEAD), F32),
        ],
        cost_estimate=pl.CostEstimate(
            flops=24 * seq * seq * q_cols, bytes_accessed=seq * q_cols * 16, transcendentals=heads * seq * seq
        ),
        name="attn_backward",
    )(starts, *q, *own, *got, *d_out, *out, lse, lo, hi, cosine, sine)


def hidden_kernel(ff, w_ref, n2_ref, df_ref, out_ref):
    dh = dot(w_ref[2 * ff :, :], df_ref[...], 1, 1)
    gu = dot(w_ref[: 2 * ff, :], n2_ref[...], 1, 1)
    gate, up = gu[:ff], gu[ff:]
    sig = jax.nn.sigmoid(gate)
    silu = gate * sig
    out_ref[:ff, :] = (dh * up * (sig * (1.0 + gate * (1.0 - sig)))).astype(BF16)
    out_ref[ff : 2 * ff, :] = (dh * silu).astype(BF16)
    out_ref[2 * ff :, :] = (silu * up).astype(BF16)


def hidden_half(w, n2, df):
    rows, width = n2.shape
    ff = w.shape[0] // 3
    tile = rows // 3
    return pl.pallas_call(
        functools.partial(hidden_kernel, ff),
        out_shape=jax.ShapeDtypeStruct((3 * ff, rows), BF16),
        grid=(rows // tile,),
        in_specs=[
            pl.BlockSpec((3 * ff, width), lambda r: (0, 0), pipeline_mode=pl.Buffered(1)),
            pl.BlockSpec((tile, width), lambda r: (r, 0)),
            pl.BlockSpec((tile, width), lambda r: (r, 0)),
        ],
        out_specs=pl.BlockSpec((3 * ff, tile), lambda r: (0, r)),
        cost_estimate=pl.CostEstimate(
            flops=6 * rows * width * ff, bytes_accessed=6 * ff * width, transcendentals=ff * rows
        ),
        name="hidden",
    )(w, n2, df)


def grads_kernel(ff, lm_ref, lo_ref, nm_ref, no_ref, dm_ref, do_ref, out_ref):
    out_ref[: 2 * ff, :] = (
        dot(lm_ref[: 2 * ff, :], nm_ref[...], 1, 0) + dot(lo_ref[: 2 * ff, :], no_ref[...], 1, 0)
    ).astype(BF16)
    out_ref[2 * ff :, :] = (
        dot(lm_ref[2 * ff :, :], dm_ref[...], 1, 0) + dot(lo_ref[2 * ff :, :], do_ref[...], 1, 0)
    ).astype(BF16)


def feed_grads(left, n2, df):
    rows, half = left[0].shape
    width = n2[0].shape[1]
    tile = 512
    whole = pl.BlockSpec((rows, half), lambda j: (0, 0), pipeline_mode=pl.Buffered(1))
    part = pl.BlockSpec((half, tile), lambda j: (0, j))
    return pl.pallas_call(
        functools.partial(grads_kernel, rows // 3),
        out_shape=jax.ShapeDtypeStruct((rows, width), BF16),
        grid=(width // tile,),
        in_specs=[whole, whole, part, part, part, part],
        out_specs=pl.BlockSpec((rows, tile), lambda j: (0, j)),
        cost_estimate=pl.CostEstimate(
            flops=4 * rows * half * width, bytes_accessed=rows * width * 2, transcendentals=0
        ),
        name="feed_grads",
    )(*left, *n2, *df)


def add_last_kernel(a0, b0, a1, b1, *rest):
    out, rows = rest[-1], b0.shape[0]
    out[:rows, :] = a0[:rows, :].astype(F32) + b0[...].astype(F32)
    out[rows:, :] = a1[:rows, :].astype(F32) + b1[...].astype(F32)


def collect_end_after(state, *others):
    one, two = state
    h, width = one.shape[0] // 2, one.shape[1]
    return pl.pallas_call(
        add_last_kernel,
        out_shape=jax.ShapeDtypeStruct((2 * h, width), F32),
        in_specs=[ANY_VMEM] * 4 + [pl.BlockSpec(memory_space=pl.ANY)] * len(others),
        out_specs=ANY_VMEM,
        name="add_last",
    )(one, side(one[h:]), two, far(two[h:]), *others)


def hold_kernel(v_ref, *rest):
    rest[-1][...] = v_ref[...]


def hold(v, *others):
    rows, width = v.shape
    tile = rows // 3 if rows % 48 == 0 else rows
    return pl.pallas_call(
        hold_kernel,
        out_shape=jax.ShapeDtypeStruct(v.shape, v.dtype),
        grid=(rows // tile,),
        in_specs=[pl.BlockSpec((tile, width), lambda i: (i, 0))] + [pl.BlockSpec(memory_space=pl.ANY)] * len(others),
        out_specs=pl.BlockSpec((tile, width), lambda i: (i, 0)),
        name="hold",
    )(v, *others)


def bring(c_ref, first, rows, refs, buf, sems):
    copies = [
        pltpu.make_async_copy(
            ref.at[pl.ds(start, rows), :], buf.at[lax.bitwise_xor(c_ref[0], bits)], sems.at[bits]
        )
        for bits, (ref, start) in enumerate(zip(refs, first))
    ]
    for copy in copies:
        copy.start()
    for copy in copies:
        copy.wait()


def finish_kernel(turned, sizes, c_ref, *refs):
    parts = len(sizes)
    pieces, out_ref, bufs, sems = refs[: 4 * parts], refs[4 * parts], refs[4 * parts + 1 : -1], refs[-1]
    for part, rows in enumerate(sizes):
        bring(c_ref, turned[1][part], rows, pieces[4 * part : 4 * part + 4], bufs[part], sems.at[part])
    at = 0
    for k in range(4):
        for part, rows in enumerate(sizes):
            v = bufs[part][k].astype(F32)
            if turned[0]:
                out_ref[:, at : at + rows] = v.T
            else:
                out_ref[at : at + rows, :] = v
            at += rows


def finish(c, sizes, turned, parts):
    width = parts[0][0][0].shape[1]
    total = 4 * sum(sizes)
    shape = (width, total) if turned else (total, width)
    firsts = [[first for _, first in part] for part in parts]
    return pl.pallas_call(
        functools.partial(finish_kernel, (turned, firsts), sizes),
        out_shape=jax.ShapeDtypeStruct(shape, F32),
        in_specs=[ANY_SMEM] + [pl.BlockSpec(memory_space=pl.ANY)] * (4 * len(parts)),
        out_specs=ANY_VMEM,
        scratch_shapes=[pltpu.VMEM((4, rows, width), BF16) for rows in sizes]
        + [pltpu.SemaphoreType.DMA((len(parts), 4))],
        name="finish",
    )(c, *[v for part in parts for v, _ in part])


def finish_attn_kernel(q_cols, c_ref, r0, r1, r2, r3, q_ref, k_ref, v_ref, o_ref, gain_ref, buf, sems):
    rows = buf.shape[1]
    bring(c_ref, (0,) * 4, rows, (r0, r1, r2, r3), buf, sems)
    qkv = q_cols + HEAD
    for k in range(4):
        q_ref[:, k * q_cols : (k + 1) * q_cols] = buf[k, :q_cols, :].astype(F32).T
        to = v_ref if k % 2 else k_ref
        to[:, (k // 2) * HEAD : (k // 2 + 1) * HEAD] = buf[k, q_cols:qkv, :].astype(F32).T
        o_ref[k * q_cols : (k + 1) * q_cols, :] = buf[k, qkv + 16 :, :].astype(F32)
    gain_ref[...] = sum(buf[k, qkv : qkv + 16, :].astype(F32) for k in range(4))


def finish_attn(c, q_cols, pieces):
    rows, width = pieces[0].shape
    shapes = [(width, 4 * q_cols), (width, 2 * HEAD), (width, 2 * HEAD), (4 * q_cols, width), (16, width)]
    return pl.pallas_call(
        functools.partial(finish_attn_kernel, q_cols),
        out_shape=tuple(jax.ShapeDtypeStruct(shape, F32) for shape in shapes),
        in_specs=[ANY_SMEM] + [pl.BlockSpec(memory_space=pl.ANY)] * 4,
        out_specs=(ANY_VMEM,) * 5,
        scratch_shapes=[pltpu.VMEM((4, rows, width), BF16), pltpu.SemaphoreType.DMA((4,))],
        name="finish_attn",
    )(c, *pieces)


def tables(c, t, core, tok_rows, seq_ids, pic_starts, pic_lengths):
    seq_len = seq_ids.shape[1]
    start_list = arrival_starts(c, t, tok_rows)
    starts = jnp.stack(start_list + [core]).astype(jnp.int32)
    positions = (starts[:16, None] + jnp.arange(seq_len // 16, dtype=jnp.int32)[None, :]).reshape(-1)
    frequency = jnp.power(rope_base, -jnp.arange(HEAD // 2, dtype=F32) * 2.0 / HEAD)
    angles = positions.astype(F32)[:, None] * frequency[None, :]
    cosine, sine = jnp.cos(angles), jnp.sin(angles)
    cosine = jnp.concatenate([cosine, cosine], axis=1)
    sine = jnp.concatenate([-sine, sine], axis=1)
    docs = seq_ids[0]
    index = jnp.arange(seq_len, dtype=jnp.int32)
    lo = jnp.sum((docs[:, None] < docs[None, :]).astype(jnp.int32), axis=0)
    doc_end = jnp.sum((docs[:, None] <= docs[None, :]).astype(jnp.int32), axis=0) - 1
    pic_ends = pic_starts[0] + pic_lengths[0]
    inside = (index[:, None] >= pic_starts[0][None, :]) & (index[:, None] < pic_ends[None, :])
    last = jnp.max(jnp.where(inside, pic_ends[None, :] - 1, -1), axis=1)
    hi = jnp.minimum(doc_end, jnp.maximum(index, last))
    lo, hi = lo[None, :], hi[None, :]
    return starts, cosine, sine, lo, hi


def body(
    tokens,
    seq_ids,
    pic_starts,
    pic_lengths,
    skip_mask,
    w_query,
    w_key,
    w_value,
    w_out,
    w_gate,
    w_up,
    w_down,
    gain_attn,
    gain_ffn,
    cotangent,
):
    tok_rows = tokens.shape[1]
    own = tok_rows // 2
    seq_len = seq_ids.shape[1]
    slot = seq_len // pic_starts.shape[1]
    c = lax.axis_index("ctx")
    t = lax.axis_index("tp")
    core = (c & 1).astype(jnp.int32)
    q_cols = w_query.shape[1] // 4
    ff = w_gate.shape[1] // 4
    part_a = (ff * 3 // 4 + 15) // 16 * 16
    part_b = ff - part_a

    flag = seq_ids[0, 0] >= 0
    qkv_cols = q_cols + HEAD
    half = seq_len // 2
    core_flag = core.reshape(1)
    first_own = pack_first(
        jnp.stack([c, core, c >> 1]).astype(jnp.int32), w_query, w_key, w_value, w_out, gain_attn, gain_ffn
    )
    first = gather_whole(first_own)

    def start_stage(tokens, skip_mask, cotangent, w_gate, w_up, w_down, seq_ids, pic_starts, pic_lengths):
        x_own_b = lax.dynamic_slice_in_dim(tokens[0], t * own, own, 0)
        keep_own = lax.dynamic_slice_in_dim(skip_mask[0], t * own, own, 0).astype(F32)[:, None]
        dy_own = lax.dynamic_slice_in_dim(cotangent[0], t * own, own, 0).astype(F32)
        parts = spread_start(x_own_b)
        wd_own = lax.dynamic_slice_in_dim(w_down, c * ff, ff, 0)
        wg_t = lax.dynamic_slice_in_dim(w_gate, c * ff, ff, 1).T
        wu_t = lax.dynamic_slice_in_dim(w_up, c * ff, ff, 1).T
        weights = [
            jnp.concatenate([v[first:last] for v in (wg_t, wu_t, wd_own)], axis=0)
            for first, last in ((0, part_a), (part_a, ff))
        ]
        parts = after(parts, weights)
        ready = parts[:2] + spread_more(parts)
        table = tables(c, t, core, tok_rows, seq_ids, pic_starts, pic_lengths)
        d_ffn_own = (keep_own * dy_own).astype(BF16)
        x_mine = spread_join(after(ready, table, d_ffn_own))
        x_other = near(x_mine)
        return x_own_b.astype(F32), keep_own, dy_own, d_ffn_own, x_mine, x_other, weights, table

    x_own, keep_own, dy_own, d_ffn_own, x_mine, x_other, weights, (starts, cosine, sine, lo, hi) = fenced(
        flag, start_stage,
        *after((tokens, skip_mask, cotangent, w_gate, w_up, w_down, seq_ids, pic_starts, pic_lengths), first_own)
    )
    weights = after(weights, x_other)
    wa, wb = gather_whole(weights[0]), gather_whole(weights[1])

    def forward_stage(x_mine, x_other, first, d_ffn_own, x_own, keep_own, cosine, sine, lo, hi, starts):
        wo = first[qkv_cols + 16 :]
        gain_two = first[qkv_cols + 1 : qkv_cols + 2].astype(F32)
        df_parts = spread_start(d_ffn_own)
        n1m, qm, kvm = qkv_half(core_flag, x_mine, first, qkv_cols, cosine[:half], sine[:half])
        n1o, qo, kvo = qkv_half(core_flag, x_other, first, qkv_cols, cosine[half:], sine[half:])
        q, own_kv = (qm, qo), (kvm, kvo)
        got = (near(kvo), near(kvm))
        q = after(q, df_parts)
        df_ready = df_parts[:2] + spread_more(df_parts)
        hm, ho, lse = attn_forward(starts, q, own_kv, got, lo, hi, slot)
        hm, ho = after((hm, ho), df_ready)
        both = join_cores(dot(hm, wo, 1, 0).astype(BF16), dot(ho, wo, 1, 0).astype(BF16))
        state = collect_first(both)
        dfm = spread_join(after(df_ready, both))
        attn = collect_end(collect_second(after(state, dfm)))
        dfo = near(dfm)
        mid = x_own + keep_own * attn
        inv_two = lax.rsqrt(jnp.mean(mid * mid, axis=-1, keepdims=True) + norm_eps)
        hat_two = mid * inv_two
        n2m, n2o = spread((hat_two * gain_two).astype(BF16))
        return n1m, n1o, q, own_kv, got, hm, ho, lse, dfm, dfo, n2m, n2o, mid, inv_two, hat_two

    n1m, n1o, q, own_kv, got, hm, ho, lse, dfm, dfo, n2m, n2o, mid, inv_two, hat_two = fenced(
        flag, forward_stage, x_mine, x_other, first, d_ffn_own, x_own, keep_own, cosine, sine, lo, hi, starts
    )

    am, ao = hidden_half(wa, n2m, dfm), hidden_half(wa, n2o, dfo)
    grad_a = feed_grads((am, ao), (n2m, n2o), (dfm, dfo))
    shard_a = scatter_whole(grad_a)
    pao = dot(ao[: 2 * part_a], wa[: 2 * part_a], 0, 0).astype(BF16)
    bm, bo = hidden_half(wb, n2m, dfm), hidden_half(wb, n2o, dfo)
    grad_b = feed_grads((bm, bo), (n2m, n2o), (dfm, dfo))
    shard_b = scatter_whole(grad_b)

    def middle_stage(am, ao, bm, bo, pao, wa, wb, first, dy_own, keep_own, hat_two, inv_two):
        gain_two = first[qkv_cols + 1 : qkv_cols + 2].astype(F32)
        p_other = (pao.astype(F32) + dot(bo[: 2 * part_b], wb[: 2 * part_b], 0, 0)).astype(BF16)
        p_mine = (
            dot(am[: 2 * part_a], wa[: 2 * part_a], 0, 0) + dot(bm[: 2 * part_b], wb[: 2 * part_b], 0, 0)
        ).astype(BF16)
        both = join_cores(p_mine, p_other)
        state = collect_first(both)
        am, ao, bm, bo = after((am, ao, bm, bo), both)

        def feed_out(a, b):
            return (
                dot(a[2 * part_a :], wa[2 * part_a :], 0, 0) + dot(b[2 * part_b :], wb[2 * part_b :], 0, 0)
            ).astype(BF16)

        f_other, f_mine = feed_out(ao, bo), feed_out(am, bm)
        d_n2 = collect_end(collect_second(after(state, f_other, f_mine)))
        d_mid = dy_own + norm_back(d_n2, hat_two, inv_two, gain_two)
        share_two = jnp.sum(d_n2 * hat_two, axis=0, keepdims=True)
        f_split = collect_split(join_cores(f_mine, f_other))
        dam, dao = spread((keep_own * d_mid).astype(BF16), f_split)
        d_head_m = dot(dam, first[qkv_cols + 16 :], 1, 1).astype(BF16)
        return d_mid, share_two, dam, dao, f_split, d_head_m

    bm, bo = after((bm, bo), grad_b)
    d_mid, share_two, dam, dao, f_split, d_head_m = fenced(
        flag, middle_stage, am, ao, bm, bo, pao, wa, wb, first, dy_own, keep_own, hat_two, inv_two
    )

    def backward_stage(
        share_two, dam, dao, f_split, d_head_m, first, q, own_kv, got, hm, ho, lse, lo, hi, cosine, sine, starts,
        x_mine, x_other, n1m, n1o, shard_a
    ):
        wqkv, wo = first[:qkv_cols], first[qkv_cols + 16 :]
        f_state = collect_send(f_split)
        d_head = (d_head_m, dot(dao, wo, 1, 1).astype(BF16))
        dqm, dqo, keepm, keepo, sendm, sendo = attn_backward(
            starts, q, own_kv, got, d_head, (hm, ho), lse, lo, hi, cosine, sine, slot
        )
        sendm, sendo = after((sendm, sendo), f_state)
        a_far = far(shard_a[: 2 * part_a])
        got_m, got_o = near(sendo), near(sendm)
        do = jnp.concatenate([dqo, (keepo + got_o.astype(F32)).astype(BF16)], axis=1)
        e_other = dot(do, wqkv, 1, 0).astype(BF16)
        dm = jnp.concatenate([dqm, (keepm + got_m.astype(F32)).astype(BF16)], axis=1)
        e_mine = dot(dm, wqkv, 1, 0).astype(BF16)
        both = join_cores(e_mine, e_other)
        state = collect_first(both)
        dm, do, hm, ho, x_mine, x_other = after((dm, do, hm, ho, x_mine, x_other), both)
        grad_qkv = (dot(dm, n1m, 0, 0) + dot(do, n1o, 0, 0)).astype(BF16)

        def gain_share(e, x):
            x = x.astype(F32)
            inv = lax.rsqrt(jnp.mean(x * x, axis=-1, keepdims=True) + norm_eps)
            return jnp.sum(e.astype(F32) * (x * inv), axis=0, keepdims=True)

        share_one = gain_share(e_mine, x_mine) + gain_share(e_other, x_other)
        shares = jnp.concatenate(
            [share_one, share_two, jnp.zeros((14, share_one.shape[1]), F32)], axis=0
        )
        shares_side = side(shares.astype(BF16))
        state = collect_second(after(state, grad_qkv, shares))
        hm, ho, dam, dao = after((hm, ho, dam, dao), state)
        grad_out = (dot(hm, dam, 0, 0) + dot(ho, dao, 0, 0)).astype(BF16)
        shares = (shares + shares_side.astype(F32)).astype(BF16)
        grad_attn = jnp.concatenate([grad_qkv, shares, grad_out], axis=0)
        d_n1 = collect_end_after(state, grad_out)
        return d_n1, grad_attn, collect_second(f_state), a_far

    d_n1, grad_attn, f_state, a_far = fenced(
        flag, backward_stage, share_two, dam, dao, f_split, d_head_m, first, q, own_kv, got, hm, ho, lse, lo, hi,
        cosine, sine, starts, x_mine, x_other, n1m, n1o, shard_a
    )
    shard_attn = scatter_whole(after(grad_attn, shard_b))
    member = c.astype(jnp.int32).reshape(1)

    def end_stage(d_n1, f_state, x_own, d_mid, first, mid, keep_own, shard_a, a_far, shard_b):
        gain_one = first[qkv_cols : qkv_cols + 1].astype(F32)
        ffn = collect_end(f_state)
        inv_one = lax.rsqrt(jnp.mean(x_own * x_own, axis=-1, keepdims=True) + norm_eps)
        hat_one = x_own * inv_one
        input_grad = (d_mid + norm_back(d_n1, hat_one, inv_one, gain_one)).astype(BF16)
        output = (mid + keep_own * ffn).astype(BF16)
        gate_far = far(hold(shard_b[:part_b], ffn))
        a_near, a_near_far, b_near = near(shard_a), near(a_far), near(shard_b)
        grad_gate = finish(
            member, sizes, True,
            [
                [(shard_a, 0), (a_near, 0), (a_far, 0), (a_near_far, 0)],
                [(shard_b, 0), (b_near, 0), (gate_far, 0), (near(gate_far), 0)],
            ],
        )
        rest = jnp.concatenate([shard_a[2 * part_a :], shard_b[part_b:]], axis=0)
        rest_far = hold(far(hold(rest, ffn)), grad_gate)
        return (
            in_order(input_grad, side(input_grad), t), output, grad_gate, a_near, a_near_far, b_near, rest_far, near(rest_far)
        )

    sizes = (part_a, part_b)
    input_grad, output, grad_gate, a_near, a_near_far, b_near, rest_far, near_far = fenced(
        flag, end_stage, d_n1, f_state, x_own, d_mid, first, mid, keep_own, shard_a, a_far, shard_b
    )

    def last_stage(shard_a, shard_b, a_near, a_far, a_near_far, b_near, rest_far, near_far, shard_attn, output):
        attn_far = far(shard_attn)
        up = [
            [(shard_a, part_a), (a_near, part_a), (a_far, part_a), (a_near_far, part_a)],
            [(shard_b, part_b), (b_near, part_b), (rest_far, part_a), (near_far, part_a)],
        ]
        down = [
            [(shard_a, 2 * part_a), (a_near, 2 * part_a), (rest_far, 0), (near_far, 0)],
            [(shard_b, 2 * part_b), (b_near, 2 * part_b), (rest_far, part_a + part_b), (near_far, part_a + part_b)],
        ]
        feed = finish(member, sizes, True, up), finish(member, sizes, False, down)
        attn_far = hold(attn_far, *feed)
        return feed, in_order(output, side(output), t), finish_attn(
            member, q_cols, (shard_attn, near(shard_attn), attn_far, near(attn_far))
        )

    (grad_up, grad_down), output, (grad_query, grad_key, grad_value, grad_out, gain_grads) = fenced(
        flag, last_stage, shard_a, shard_b, a_near, a_far, a_near_far, b_near, rest_far, near_far, shard_attn, output
    )
    return (
        output[None],
        input_grad[None],
        grad_query,
        grad_key,
        grad_value,
        grad_out,
        grad_gate,
        grad_up,
        grad_down,
        gain_grads[0],
        gain_grads[1],
    )


def solution(mesh):
    placed = (
        P("fsdp", "ctx", None),
        P("fsdp", None),
        P("fsdp", None),
        P("fsdp", None),
        P("fsdp", "ctx"),
        P("fsdp", "tp"),
        P("fsdp", "tp"),
        P("fsdp", "tp"),
        P("tp", "fsdp"),
        P("fsdp", "tp"),
        P("fsdp", "tp"),
        P("tp", "fsdp"),
        P("fsdp"),
        P("fsdp"),
        P("fsdp", "ctx", None),
    )
    return jax.shard_map(
        body,
        mesh=mesh,
        in_specs=placed,
        out_specs=(
            P("fsdp", "ctx", None),
            P("fsdp", "ctx", None),
            P("fsdp", "tp"),
            P("fsdp", "tp"),
            P("fsdp", "tp"),
            P("tp", "fsdp"),
            P("fsdp", "tp"),
            P("fsdp", "tp"),
            P("tp", "fsdp"),
            P("fsdp"),
            P("fsdp"),
        ),
        check_vma=False,
    )
```
